128 devices in a mesh: lat: 16 (over x, z), lon: 8 (over y, core).
Axes of the slice: x: 4, y: 4, z: 4, core: 2. Of those that a mesh axis runs over, the one named last changes fastest.
Arguments:
- thickness: float32 [2, 2048, 8192], P(None, 'lat', 'lon'), may hold values from 0.5 to 1.5
- winds: float32 [2, 2, 2048, 8192], P(None, None, 'lat', 'lon'), may hold values from -3 to 3
- terrain: float32 [2048, 8192], P('lat', 'lon'), may hold values from -1.5 to 1.5
- cutoffs: int32 [682], replicated, may hold values from 1 to 4096, as said below
Outputs:
- new_thickness: float32 [2, 2048, 8192], P(None, 'lat', 'lon')
- new_winds: float32 [2, 2, 2048, 8192], P(None, None, 'lat', 'lon')
The draws below stay inside these ranges and needn't reach their ends.
Inputs may be any that keep to these rules, and one draw needn't show every extreme that they name: cutoffs[p] is the count of the lowest zonal wavenumbers kept on cap row p (the 341 southernmost rows from south to north, then the 341 northernmost).
All inputs are finite; a program needn't handle non-finite values.
Results may differ from the reference program's by a relative error of at most 0.0003.
Values sent between devices are 32-bit elements; how exact they have to be, the bound alone decides.
No kernel may reach another device: no remote copies, remote signals or barrier semaphores. Data moves between devices by JAX's collectives and lax.ppermute only.
A program may use at most 128 MiB of HBM per device.

```python
import math
import jax
import jax.numpy as jnp
from jax import lax

ROWS_DEV = 128
NLON = 8192
LEVELS = 2
STEPS = 1
NLAT = 2048
POLAR_ROWS = 341
N_LAT = 16


def draw_cutoffs(key, part):
    offsets = jnp.arange(POLAR_ROWS, dtype=jnp.int32)
    distance = jnp.concatenate([offsets, POLAR_ROWS - 1 - offsets])
    nyquist = NLON // 2
    ceiling = 1 + (nyquist - 1) * distance // max(POLAR_ROWS - 1, 1)
    jitter = jax.random.randint(key, (2 * POLAR_ROWS,), 0, 1048576, dtype=jnp.int32)
    lowered = ceiling - jitter % (ceiling // 2 + 1)
    return jnp.where(distance == POLAR_ROWS - 1, ceiling, lowered).astype(jnp.int32)


def levels(key, dims, shards, least, top_value):
    def one(position, parts):
        steps = jax.random.uniform(jax.random.fold_in(jax.random.fold_in(key, 6), position), (parts,), jnp.float32, least / len(shards), top_value / len(shards))
        return jnp.repeat(jnp.exp(steps), dims[position] // parts).reshape((-1,) + (1,) * (len(dims) - position - 1))

    level = one(*shards[0])
    for cut in shards[1:]:
        level = level * one(*cut)
    return level


def bell_draw(stream_key, shape, width, limit, split=(), kind=jnp.bfloat16):
    entries = width * jax.random.normal(stream_key, shape, jnp.float32)
    if split:
        entries = entries * levels(stream_key, shape, split, -0.22, 0.18)
    return jnp.clip(entries, -limit, limit).astype(kind)


def setup_inputs(seed: int = 0) -> dict:
    key_list = jax.random.split(jax.random.key(seed), 5)
    return {
        "thickness": jnp.clip(0.5 + 1.0 * jax.random.uniform(key_list[0], (LEVELS, NLAT, NLON), jnp.float32) ** levels(key_list[0], (LEVELS, NLAT, NLON), ((1, 16), (2, 8)), -0.2, 0.2), 0.5, 1.5),
        "winds": bell_draw(key_list[1], (2, LEVELS, NLAT, NLON), 0.5, 3.0, ((2, 16), (3, 8)), jnp.float32),
        "terrain": bell_draw(key_list[2], (NLAT, NLON), 0.3, 1.5, ((0, 16), (1, 8)), jnp.float32),
        "cutoffs": draw_cutoffs(jax.random.fold_in(key_list[4], 71), 0),
    }


GRAVITY = 1.0
DENSITY_RATIO = 0.9
CORIOLIS = 1.0


def stencil_tendency(padded, row_start, total_rows, circle):
    row_count = padded.shape[1] - 2
    thickness = padded[0:2]
    zonal_wind = padded[2:4]
    ground = padded[6]
    row_ids = row_start - 1 + jnp.arange(row_count + 2, dtype=jnp.int32)
    spacing = math.pi / total_rows
    centre_lat = -0.5 * math.pi + (row_ids.astype(jnp.float32) + 0.5) * spacing
    face_lat = -0.5 * math.pi + (row_ids.astype(jnp.float32) + 1.0) * spacing
    face_live = jnp.where((row_ids >= 0) & (row_ids < total_rows - 1), 1.0, 0.0).astype(jnp.float32)
    centre_cos = jnp.cos(centre_lat)
    face_cos = jnp.cos(face_lat) * face_live
    face_inverse = face_live / (face_cos + (1.0 - face_live))
    merid_step = circle / (2.0 * total_rows)
    merid_wind = padded[4:6] * face_live[None, :, None]
    inner_cosine = centre_cos[1:-1][None, :, None]

    flux_east = 0.5 * (thickness[:, :, :-1] + thickness[:, :, 1:]) * zonal_wind[:, :, :-1]
    flux_north = 0.5 * (thickness[:, :-1, :] + thickness[:, 1:, :]) * merid_wind[:, :-1, :] * face_cos[:-1][None, :, None]
    converge = (flux_east[:, 1:-1, 1:] - flux_east[:, 1:-1, :-1]) + (flux_north[:, 1:, 1:-1] - flux_north[:, :-1, 1:-1]) / merid_step
    thick_tend = -converge / inner_cosine

    kinetic = 0.25 * (zonal_wind[:, 1:, 1:] ** 2 + zonal_wind[:, 1:, :-1] ** 2 + merid_wind[:, 1:, 1:] ** 2 + merid_wind[:, :-1, 1:] ** 2)
    upper_layer = thickness[0, 1:, 1:]
    lower_layer = thickness[1, 1:, 1:]
    surface = ground[1:, 1:]
    potential = jnp.stack([GRAVITY * (upper_layer + lower_layer + surface), GRAVITY * (DENSITY_RATIO * upper_layer + lower_layer + surface)])
    energy = kinetic + potential

    merid_diff = merid_wind[:, :-1, 1:] - merid_wind[:, :-1, :-1]
    zonal_diff = zonal_wind[:, 1:, :-1] * centre_cos[1:][None, :, None] - zonal_wind[:, :-1, :-1] * centre_cos[:-1][None, :, None]
    absolute = CORIOLIS * jnp.sin(face_lat[:-1])[None, :, None] + (merid_diff - zonal_diff / merid_step) * face_inverse[:-1][None, :, None]

    merid_mean = 0.25 * (merid_wind[:, 1:-1, 1:-1] + merid_wind[:, 1:-1, 2:] + merid_wind[:, :-2, 1:-1] + merid_wind[:, :-2, 2:])
    zonal_mean = 0.25 * (zonal_wind[:, 1:-1, 1:-1] + zonal_wind[:, 1:-1, :-2] + zonal_wind[:, 2:, 1:-1] + zonal_wind[:, 2:, :-2])
    centre_energy = energy[:, :-1, :-1]
    east_energy = energy[:, :-1, 1:]
    north_energy = energy[:, 1:, :-1]
    zonal_tend = 0.5 * (absolute[:, 1:, 1:] + absolute[:, :-1, 1:]) * merid_mean - (east_energy - centre_energy) / inner_cosine
    merid_tend = (-0.5 * (absolute[:, 1:, 1:] + absolute[:, 1:, :-1]) * zonal_mean - (north_energy - centre_energy) / merid_step) * face_live[1:-1][None, :, None]
    return jnp.concatenate([thick_tend, zonal_tend, merid_tend], axis=0)


def full_tendency(state, terrain):
    padded_state = jnp.pad(state, ((0, 0), (1, 1), (0, 0)))
    padded_ground = jnp.pad(terrain, ((1, 1), (0, 0)))

    def one_band(index):
        anchor = (index * ROWS_DEV).astype(jnp.int32)
        block = lax.dynamic_slice_in_dim(padded_state, anchor, ROWS_DEV + 2, axis=1)
        ground = lax.dynamic_slice_in_dim(padded_ground, anchor, ROWS_DEV + 2, axis=0)
        stacked = jnp.concatenate([block, ground[None]], axis=0)
        wrapped = jnp.concatenate([stacked[:, :, -1:], stacked, stacked[:, :, :1]], axis=2)
        return stencil_tendency(wrapped, anchor, NLAT, NLON)

    pieces = lax.map(one_band, jnp.arange(N_LAT, dtype=jnp.int32))
    return jnp.transpose(pieces, (1, 0, 2, 3)).reshape(6, NLAT, NLON)


def polar_filter(tendency, cutoffs):
    caps = jnp.concatenate([tendency[:, :POLAR_ROWS], tendency[:, NLAT - POLAR_ROWS:]], axis=1)
    spectrum = jnp.fft.rfft(caps, axis=-1)
    wavenumber = jnp.arange(NLON // 2 + 1, dtype=jnp.int32)
    keep = wavenumber[None, :] < cutoffs[:, None]
    caps = jnp.fft.irfft(jnp.where(keep[None], spectrum, 0.0), n=NLON, axis=-1).astype(jnp.float32)
    middle = tendency[:, POLAR_ROWS:NLAT - POLAR_ROWS]
    return jnp.concatenate([caps[:, :POLAR_ROWS], middle, caps[:, POLAR_ROWS:]], axis=1)


def reference(thickness, winds, terrain, cutoffs):
    live = jnp.where(jnp.arange(NLAT, dtype=jnp.int32) < NLAT - 1, 1.0, 0.0).astype(jnp.float32)
    current = jnp.concatenate([thickness, winds[0], winds[1] * live[None, :, None]], axis=0)
    step_size = 0.1 * min(1.0, NLON / (2.0 * NLAT))
    for step_index in range(STEPS):
        anchor = current
        for fraction in (1.0 / 3.0, 0.5, 1.0):
            tendency = polar_filter(full_tendency(current, terrain), cutoffs)
            current = anchor + (fraction * step_size) * tendency
    return current[0:2], current[2:6].reshape(2, 2, NLAT, NLON)
```

```python
import functools
import math

import jax
import jax.numpy as jnp
import ml_dtypes
import numpy as np
from jax import lax
from jax.experimental import pallas as pl
from jax.experimental.pallas import tpu as pltpu
from jax.sharding import PartitionSpec as P

DENSITY_RATIO = 0.9
HALO = 3
SUB = 8
LANES = 128
RADIX = 64
HALF = RADIX // 2
SPEC_BLOCKS = HALF + 2
UNCUT = 1 << 20
TILE_ROWS = 128
PAIR = 16
COEFS = 7


def twisted(real, imag, k, n):
    angle = 2.0 * math.pi * k / n
    c, s = math.cos(angle), math.sin(angle)
    if k == 0:
        return real, imag
    if 8 * k == n:
        return (real + imag) * c, (imag - real) * c
    if 8 * k == 3 * n:
        return (imag - real) * s, -(real + imag) * s
    return real * c + imag * s, imag * c - real * s


def real_fft(x):
    n = len(x)
    if n == 1:
        return [x[0]], [None]
    er, ei = real_fft(x[0::2])
    odr, odi = real_fft(x[1::2])
    half = n // 2
    re, im = [None] * (half + 1), [None] * (half + 1)
    re[0], re[half] = er[0] + odr[0], er[0] - odr[0]
    for k in range(1, half // 2 + 1):
        if 2 * k == half:
            re[k], im[k] = er[k], -odr[k]
            continue
        tr, ti = twisted(odr[k], odi[k], k, n)
        re[k], im[k] = er[k] + tr, ei[k] + ti
        re[half - k], im[half - k] = er[k] - tr, ti - ei[k]
    return re, im


def real_ifft(re, im):
    n = 2 * (len(re) - 1)
    if n == 0:
        return [re[0]]
    half = n // 2
    if n == 2:
        return [re[0] + re[1], re[0] - re[1]]
    quarter = half // 2
    er, ei = [None] * (quarter + 1), [None] * (quarter + 1)
    odr, odi = [None] * (quarter + 1), [None] * (quarter + 1)
    er[0], odr[0] = re[0] + re[half], re[0] - re[half]
    for k in range(1, quarter + 1):
        if k == quarter:
            er[k], odr[k] = 2.0 * re[k], -2.0 * im[k]
            continue
        sr, si = re[k] + re[half - k], im[k] - im[half - k]
        dr, di = re[k] - re[half - k], im[k] + im[half - k]
        er[k], ei[k] = sr, si
        odi[k], odr[k] = twisted(di, dr, k, n)
    even = real_ifft(er, ei)
    odd = real_ifft(odr, odi)
    out = [None] * n
    out[0::2], out[1::2] = even, odd
    return out


def filter_tables():
    b = np.arange(LANES)
    angle = 2.0 * np.pi * (np.outer(b, b) % LANES) / LANES
    c, s = np.cos(angle), np.sin(angle)
    forward = np.block([[c, -s], [s, c]])
    backward = forward.T / (RADIX * LANES)

    def split(w):
        hi = w.astype(np.float32).astype(ml_dtypes.bfloat16)
        lo = (w - hi.astype(np.float64)).astype(np.float32).astype(ml_dtypes.bfloat16)
        return hi, lo

    k1 = np.arange(40)[:, None]
    twist = 2.0 * np.pi * k1 * b[None, :] / (RADIX * LANES)
    return (
        *split(forward),
        *split(backward),
        np.cos(twist).astype(np.float32),
        np.sin(twist).astype(np.float32),
    )


def pack_kernel(bands, lat_ref, th_ref, wi_ref, te_ref, south_ref, north_ref, out_ref):
    groups = out_ref.shape[0]
    height = out_ref.shape[2] // SUB
    own = height - 2 * HALO
    rows = groups * own

    def put(g, f, dst, count, read):
        for s in range(SUB):
            out_ref[g, f, pl.ds(dst * SUB + s, count, stride=SUB), :] = read(s)

    for f in range(7):
        if f < 2:
            src = th_ref.at[f]
        elif f < 6:
            src = wi_ref.at[f - 2]
        else:
            src = te_ref

        def rows_of(start, count, src=src):
            return lambda s: src[pl.ds(start, count), s * LANES : (s + 1) * LANES]

        for g in range(groups):
            for m in range(own // SUB):
                put(g, f, HALO + m * SUB, SUB, rows_of(g * own + m * SUB, SUB))
            if g > 0:
                put(g, f, 0, HALO, rows_of(g * own - HALO, HALO))
            else:
                put(g, f, 0, HALO, lambda s, f=f: south_ref[f, :, s * LANES : (s + 1) * LANES])
            if g < groups - 1:
                put(g, f, HALO + own, HALO, rows_of((g + 1) * own, HALO))
            else:
                put(g, f, HALO + own, HALO, lambda s, f=f: north_ref[f, :, s * LANES : (s + 1) * LANES])

    @pl.when(lat_ref[0] == bands - 1)
    def _():
        for f in (4, 5):
            out_ref[groups - 1, f, pl.ds((HALO + own - 1) * SUB, SUB), :] = jnp.zeros((SUB, LANES), jnp.float32)


def unpack_kernel(in_ref, th_ref, wi_ref):
    groups = in_ref.shape[0]
    own = in_ref.shape[2] // SUB
    for f in range(6):
        dst = th_ref.at[f] if f < 2 else wi_ref.at[f - 2]
        for g in range(groups):
            for m in range(own // SUB):
                for s in range(SUB):
                    dst[pl.ds(g * own + m * SUB, SUB), s * LANES : (s + 1) * LANES] = in_ref[
                        g, f, pl.ds(m * SUB * SUB + s, SUB, stride=SUB), :
                    ]


def step_kernel(
    merid_step,
    step_size,
    coef,
    flags,
    x_ref,
    cut_ref,
    wfh_ref,
    wfl_ref,
    wbh_ref,
    wbl_ref,
    twc_ref,
    tws_ref,
    out_ref,
    s_ref,
    t_ref,
    e_ref,
    z_ref,
    uu_ref,
    vv_ref,
    y_ref,
):
    chunks = x_ref.shape[0]
    height = x_ref.shape[1] // 7
    own = height - 2 * HALO
    lane = lax.broadcasted_iota(jnp.int32, (SUB, LANES), 1)
    sub = lax.broadcasted_iota(jnp.int32, (SUB, LANES), 0)
    last_lane, first_lane = lane == LANES - 1, lane == 0
    last_sub, first_sub = sub == SUB - 1, sub == 0
    dy_inv = 1.0 / merid_step

    def east(xs):
        y = [pltpu.roll(x, LANES - 1, 1) for x in xs]
        r = [pltpu.roll(v, SUB - 1, 0) for v in y]
        return [
            jnp.where(last_lane, jnp.where(last_sub, r[(d + 1) % chunks], r[d]), y[d])
            for d in range(chunks)
        ]

    def west(xs):
        y = [pltpu.roll(x, 1, 1) for x in xs]
        r = [pltpu.roll(v, 1, 0) for v in y]
        return [
            jnp.where(first_lane, jnp.where(first_sub, r[d - 1], r[d]), y[d]) for d in range(chunks)
        ]

    def stage(src, in_lo, fraction, final):
        in_hi = height - 1 - in_lo
        lo, hi = in_lo + 1, in_hi - 1
        count = hi - lo + 1

        def get(f, r):
            return [src[d, f * height + r] for d in range(chunks)]

        def terrain(r):
            return [x_ref[d, 6 * height + r] for d in range(chunks)]

        def corners(r, carry):
            rn = jnp.minimum(r + 1, in_hi)
            rs = jnp.maximum(r - 1, in_lo)
            c_half, cn_half = coef[0, r] * dy_inv, coef[0, rn] * dy_inv
            e_inv, sine = coef[2, r], coef[3, r]
            h0, h1, ground = get(0, r), get(1, r), terrain(r)
            base = [a + b for a, b in zip(h1, ground)]
            for k in range(2):
                u, v = get(2 + k, r), get(4 + k, r)
                uw, ve = west(u), east(v)
                un, vs = get(2 + k, rn), get(4 + k, rs)
                for d in range(chunks):
                    at = (r * 2 + k) * chunks + d
                    uu_ref[at] = u[d] + uw[d]
                    vv_ref[at] = v[d] + ve[d]
                    kin = 0.25 * (u[d] * u[d] + uw[d] * uw[d] + (v[d] * v[d] + vs[d] * vs[d]))
                    e_ref[at] = kin + (base[d] + (h0[d] if k == 0 else DENSITY_RATIO * h0[d]))
                    curl = (ve[d] - v[d]) - (un[d] * cn_half - u[d] * c_half)
                    z_ref[at] = sine + curl * e_inv
            return carry

        lax.fori_loop(in_lo, in_hi + 1, corners, 0)

        def tendencies(r, carry):
            c_inv = coef[1, r]
            fn, fs = coef[4, r] * (0.5 * dy_inv), coef[4, r - 1] * (0.5 * dy_inv)
            live = coef[5, r]
            for k in range(2):

                def face(ref, row):
                    return [ref[(row * 2 + k) * chunks + d] for d in range(chunks)]

                h, hn, hs = get(k, r), get(k, r + 1), get(k, r - 1)
                u, v, vs = get(2 + k, r), get(4 + k, r), get(4 + k, r - 1)
                he = east(h)
                fx = [0.5 * (h[d] + he[d]) * u[d] for d in range(chunks)]
                fxw = west(fx)
                en, ec = face(e_ref, r + 1), face(e_ref, r)
                ee = east(ec)
                z, zs = face(z_ref, r), face(z_ref, r - 1)
                zw = west(z)
                uu, uun = face(uu_ref, r), face(uu_ref, r + 1)
                vv, vvs = face(vv_ref, r), face(vv_ref, r - 1)
                for d in range(chunks):

                    def at(f):
                        return pl.ds(
                            pl.multiple_of((d * TILE_ROWS + f * count + (r - lo)) * SUB, SUB), SUB
                        )

                    north = (h[d] + hn[d]) * (v[d] * fn) - (h[d] + hs[d]) * (vs[d] * fs)
                    t_ref[at(k), :] = ((fxw[d] - fx[d]) - north) * c_inv
                    t_ref[at(2 + k), :] = (0.125 * (z[d] + zs[d])) * (vv[d] + vvs[d]) - (ee[d] - ec[d]) * c_inv
                    t_ref[at(4 + k), :] = live * (
                        (-0.125 * (z[d] + zw[d])) * (uu[d] + uun[d]) - dy_inv * (en[d] - ec[d])
                    )
            return carry

        lax.fori_loop(lo, hi + 1, tendencies, 0)

        def circle_filter(p, carry):
            @pl.when(flags[in_lo, p] > 0)
            def _():
                def place(a, half):
                    d, s = a // SUB, a % SUB
                    start = (d * TILE_ROWS + p * PAIR + half * SUB) * SUB + s
                    return pl.ds(start, SUB, stride=SUB)

                for half in range(2):
                    re, im = real_fft([t_ref[place(a, half), :] for a in range(RADIX)])
                    for k in range(HALF + 1):
                        c, s = twc_ref[k : k + 1, :], tws_ref[k : k + 1, :]
                        if im[k] is None:
                            yr, yi = (re[k], jnp.zeros_like(re[k])) if k == 0 else (re[k] * c, -(re[k] * s))
                        else:
                            yr, yi = re[k] * c + im[k] * s, im[k] * c - re[k] * s
                        at = pl.ds((k * 2 + half) * SUB, SUB)
                        y_ref[at, 0:LANES] = yr
                        y_ref[at, LANES : 2 * LANES] = yi
                cut = cut_ref[in_lo, pl.ds(pl.multiple_of(p * PAIR, PAIR), PAIR), :]
                cut2 = jnp.concatenate([cut, cut], axis=1)
                wave = lax.broadcasted_iota(jnp.int32, (PAIR, 2 * LANES), 1)
                wave = RADIX * jnp.where(wave >= LANES, wave - LANES, wave)

                def product(y, whi, wlo):
                    hi_part = y.astype(jnp.bfloat16)
                    lo_part = (y - hi_part.astype(jnp.float32)).astype(jnp.bfloat16)
                    dot = functools.partial(jnp.dot, preferred_element_type=jnp.float32)
                    return dot(hi_part, whi) + (dot(lo_part, whi) + dot(hi_part, wlo))

                block = 3
                for start in range(0, HALF + 1, block):
                    rows = slice(start * PAIR, (start + block) * PAIR)
                    spec = product(y_ref[rows, :], wfh_ref[...], wfl_ref[...])
                    keep = []
                    for k in range(start, start + block):
                        folded = jnp.minimum(wave + k, RADIX * LANES - k - wave)
                        keep.append(folded < cut2)
                    spec = jnp.where(jnp.concatenate(keep, axis=0), spec, 0.0)
                    y_ref[rows, :] = product(spec, wbh_ref[...], wbl_ref[...])
                for half in range(2):
                    re, im = [], []
                    for k in range(HALF + 1):
                        c, s = twc_ref[k : k + 1, :], tws_ref[k : k + 1, :]
                        at = pl.ds((k * 2 + half) * SUB, SUB)
                        yr = y_ref[at, 0:LANES]
                        if k == 0:
                            re.append(yr)
                            im.append(None)
                            continue
                        yi = y_ref[at, LANES : 2 * LANES]
                        re.append(yr * c - yi * s)
                        im.append(None if k == HALF else yr * s + yi * c)
                    circles = real_ifft(re, im)
                    polar = cut[half * SUB : (half + 1) * SUB] < UNCUT
                    for a in range(RADIX):
                        at = place(a, half)
                        t_ref[at, :] = jnp.where(polar, circles[a], t_ref[at, :])

            return carry

        lax.fori_loop(0, -(-6 * count // PAIR), circle_filter, 0)

        def update(r, carry):
            inside = coef[6, r]
            for f in range(6):
                for d in range(chunks):
                    at = pl.ds(pl.multiple_of((d * TILE_ROWS + f * count + (r - lo)) * SUB, SUB), SUB)
                    value = inside * (x_ref[d, f * height + r] + (fraction * step_size) * t_ref[at, :])
                    if final:
                        out_ref[d, f * own + (r - HALO)] = value
                    else:
                        s_ref[d, f * height + r] = value
            return carry

        lax.fori_loop(lo, hi + 1, update, 0)

    stage(x_ref, 0, 1.0 / 3.0, False)
    stage(s_ref, 1, 0.5, False)
    stage(s_ref, 2, 1.0, True)


def row_tables(cutoffs, row_start, height, total_rows, polar):
    row_ids = row_start - HALO + jnp.arange(height, dtype=jnp.int32)
    spacing = math.pi / total_rows
    centre_lat = -0.5 * math.pi + (row_ids.astype(jnp.float32) + 0.5) * spacing
    face_lat = -0.5 * math.pi + (row_ids.astype(jnp.float32) + 1.0) * spacing
    inside = jnp.where((row_ids >= 0) & (row_ids < total_rows), 1.0, 0.0).astype(jnp.float32)
    live = jnp.where((row_ids >= 0) & (row_ids < total_rows - 1), 1.0, 0.0).astype(jnp.float32)
    centre_cos = jnp.cos(centre_lat)
    face_cos = jnp.cos(face_lat) * live
    face_inverse = live / (face_cos + (1.0 - live))
    coef = jnp.stack(
        [centre_cos, 1.0 / centre_cos, face_inverse, jnp.sin(face_lat), face_cos, live, inside]
    )
    capped = ((row_ids >= 0) & (row_ids < polar)) | (
        (row_ids >= total_rows - polar) & (row_ids < total_rows)
    )
    position = jnp.where(row_ids < polar, row_ids, row_ids - (total_rows - 2 * polar))
    table_ids = jnp.arange(2 * polar, dtype=jnp.int32)
    cut = jnp.sum(
        jnp.where(position[:, None] == table_ids[None, :], cutoffs[None, :], 0), axis=1, dtype=jnp.int32
    )
    cut = jnp.where(capped, cut, UNCUT)
    stages = []
    for in_lo in range(3):
        rows = jnp.tile(cut[in_lo + 1 : height - 1 - in_lo], 6)
        stages.append(jnp.pad(rows, (0, TILE_ROWS - rows.shape[0]), constant_values=UNCUT))
    cuts = jnp.stack(stages)
    flags = jnp.any(cuts.reshape(3, TILE_ROWS // PAIR, PAIR) < UNCUT, axis=2).astype(jnp.int32)
    return coef, flags, jnp.broadcast_to(cuts[:, :, None], (3, TILE_ROWS, LANES))


def body(thickness, winds, terrain, cutoffs):
    row_count, col_count = thickness.shape[1], thickness.shape[2]
    bands, sectors = lax.axis_size("lat"), lax.axis_size("lon")
    total_rows, circle = row_count * bands, col_count * sectors
    polar = (total_rows + 2) // 6
    own = row_count // sectors
    height = own + 2 * HALO
    merid_step = circle / (2.0 * total_rows)
    step_size = 0.1 * min(1.0, merid_step)
    lat = lax.axis_index("lat")
    flat = winds.reshape(4, row_count, col_count)

    tail = jnp.concatenate(
        [thickness[:, -HALO:], flat[:, -HALO:], terrain[None, -HALO:]], axis=0
    )
    head = jnp.concatenate([thickness[:, :HALO], flat[:, :HALO], terrain[None, :HALO]], axis=0)
    south = lax.ppermute(tail, "lat", [(i, i + 1) for i in range(bands - 1)])
    north = lax.ppermute(head, "lat", [(i + 1, i) for i in range(bands - 1)])

    vmem = pl.BlockSpec(memory_space=pltpu.VMEM)
    smem = pl.BlockSpec(memory_space=pltpu.SMEM)
    packed = pl.pallas_call(
        functools.partial(pack_kernel, bands),
        out_shape=jax.ShapeDtypeStruct((sectors, 7, height * SUB, LANES), jnp.float32),
        in_specs=[smem] + [vmem] * 5,
        out_specs=vmem,
        compiler_params=pltpu.CompilerParams(vmem_limit_bytes=40 << 20),
        name="pack",
    )(lat.reshape(1).astype(jnp.int32), thickness, flat, terrain, south, north)
    circles = lax.all_to_all(packed, "lon", 0, 0)

    row_start = lat * row_count + lax.axis_index("lon") * own
    coef, flags, cuts = row_tables(cutoffs, row_start, height, total_rows, polar)
    tables = [jnp.asarray(t) for t in filter_tables()]
    stepped = pl.pallas_call(
        functools.partial(step_kernel, merid_step, step_size),
        out_shape=jax.ShapeDtypeStruct((sectors, 6 * own, SUB, LANES), jnp.float32),
        in_specs=[smem, smem] + [vmem] * 8,
        out_specs=vmem,
        scratch_shapes=[
            pltpu.VMEM((sectors, 6 * height, SUB, LANES), jnp.float32),
            pltpu.VMEM((sectors * TILE_ROWS * SUB, LANES), jnp.float32),
        ]
        + [pltpu.VMEM((height * 2 * sectors, SUB, LANES), jnp.float32)] * 4
        + [pltpu.VMEM(((HALF + 1) * PAIR, 2 * LANES), jnp.float32)],
        compiler_params=pltpu.CompilerParams(vmem_limit_bytes=56 << 20),
        name="step",
    )(coef, flags, circles.reshape(sectors, 7 * height, SUB, LANES), cuts, *tables)
    returned = lax.all_to_all(stepped.reshape(sectors, 6, own * SUB, LANES), "lon", 0, 0)
    new_thickness, new_winds = pl.pallas_call(
        unpack_kernel,
        out_shape=(
            jax.ShapeDtypeStruct(thickness.shape, jnp.float32),
            jax.ShapeDtypeStruct(flat.shape, jnp.float32),
        ),
        in_specs=[vmem],
        out_specs=(vmem, vmem),
        compiler_params=pltpu.CompilerParams(vmem_limit_bytes=40 << 20),
        name="unpack",
    )(returned)
    return new_thickness, new_winds.reshape(winds.shape)


def solution(mesh):
    in_specs = (P(None, "lat", "lon"), P(None, None, "lat", "lon"), P("lat", "lon"), P())
    out_specs = (P(None, "lat", "lon"), P(None, None, "lat", "lon"))
    return jax.shard_map(body, mesh=mesh, in_specs=in_specs, out_specs=out_specs, check_vma=False)
```

```python
import functools
import math

import jax
import jax.numpy as jnp
import ml_dtypes
import numpy as np
from jax import lax
from jax.experimental import pallas as pl
from jax.experimental.pallas import tpu as pltpu
from jax.sharding import PartitionSpec as P

DENSITY_RATIO = 0.9
HALO = 3
SUB = 8
LANES = 128
RADIX = 64
HALF = RADIX // 2
SPEC_BLOCKS = HALF + 2
UNCUT = 1 << 20
TILE_ROWS = 128
PAIR = 16
UNITS = 2
BLOCK = 11
COEFS = 7


def twisted(real, imag, k, n):
    angle = 2.0 * math.pi * k / n
    c, s = math.cos(angle), math.sin(angle)
    if k == 0:
        return real, imag
    if 8 * k == n:
        return (real + imag) * c, (imag - real) * c
    if 8 * k == 3 * n:
        return (imag - real) * s, -(real + imag) * s
    return real * c + imag * s, imag * c - real * s


def real_fft(x):
    n = len(x)
    if n == 1:
        return [x[0]], [None]
    er, ei = real_fft(x[0::2])
    odr, odi = real_fft(x[1::2])
    half = n // 2
    re, im = [None] * (half + 1), [None] * (half + 1)
    re[0], re[half] = er[0] + odr[0], er[0] - odr[0]
    for k in range(1, half // 2 + 1):
        if 2 * k == half:
            re[k], im[k] = er[k], -odr[k]
            continue
        tr, ti = twisted(odr[k], odi[k], k, n)
        re[k], im[k] = er[k] + tr, ei[k] + ti
        re[half - k], im[half - k] = er[k] - tr, ti - ei[k]
    return re, im


def real_ifft(re, im):
    n = 2 * (len(re) - 1)
    if n == 0:
        return [re[0]]
    half = n // 2
    if n == 2:
        return [re[0] + re[1], re[0] - re[1]]
    quarter = half // 2
    er, ei = [None] * (quarter + 1), [None] * (quarter + 1)
    odr, odi = [None] * (quarter + 1), [None] * (quarter + 1)
    er[0], odr[0] = re[0] + re[half], re[0] - re[half]
    for k in range(1, quarter + 1):
        if k == quarter:
            er[k], odr[k] = 2.0 * re[k], -2.0 * im[k]
            continue
        sr, si = re[k] + re[half - k], im[k] - im[half - k]
        dr, di = re[k] - re[half - k], im[k] + im[half - k]
        er[k], ei[k] = sr, si
        odi[k], odr[k] = twisted(di, dr, k, n)
    even = real_ifft(er, ei)
    odd = real_ifft(odr, odi)
    out = [None] * n
    out[0::2], out[1::2] = even, odd
    return out


def filter_tables():
    b = np.arange(LANES)
    angle = 2.0 * np.pi * (np.outer(b, b) % LANES) / LANES
    c, s = np.cos(angle), np.sin(angle)
    forward = np.block([[c, -s], [s, c]])
    backward = forward.T / (RADIX * LANES)

    def split(w):
        hi = w.astype(np.float32).astype(ml_dtypes.bfloat16)
        lo = (w - hi.astype(np.float64)).astype(np.float32).astype(ml_dtypes.bfloat16)
        return hi, lo

    k1 = np.arange(40)[:, None]
    twist = 2.0 * np.pi * k1 * b[None, :] / (RADIX * LANES)
    return (
        *split(forward),
        *split(backward),
        np.cos(twist).astype(np.float32),
        np.sin(twist).astype(np.float32),
    )


def edge_kernel(th_ref, wi_ref, te_ref, tail_ref, head_ref, tile_ref, sems):
    rows = te_ref.shape[0]

    def copies(f):
        src = th_ref.at[f] if f < 2 else wi_ref.at[f - 2] if f < 6 else te_ref
        return [
            pltpu.make_async_copy(src.at[pl.ds(start, SUB)], tile_ref.at[i, f], sems.at[i, f])
            for i, start in enumerate((rows - SUB, 0))
        ]

    for f in range(7):
        for copy in copies(f):
            copy.start()
    for f in range(7):
        for i, copy in enumerate(copies(f)):
            copy.wait()
            out_ref, start = ((tail_ref, SUB - HALO), (head_ref, 0))[i]
            for s in range(SUB):
                out_ref[pl.ds(f * SUB + s, HALO, stride=7 * SUB), :] = tile_ref[
                    i, f, start : start + HALO, s * LANES : (s + 1) * LANES
                ]


def pack_kernel(bands, lat_ref, th_ref, wi_ref, te_ref, out_ref, piece_ref, sems):
    groups = out_ref.shape[0]
    height = out_ref.shape[1] // (7 * SUB)
    own = height - 2 * HALO

    for g in range(groups):
        for f in range(7):
            src = th_ref.at[f] if f < 2 else wi_ref.at[f - 2] if f < 6 else te_ref

            def put(dst, start, count):
                for s in range(SUB):
                    piece_ref[g, pl.ds((dst * 7 + f) * SUB + s, count, stride=7 * SUB), :] = src[
                        pl.ds(start, count), s * LANES : (s + 1) * LANES
                    ]

            for m in range(own // SUB):
                put(HALO + m * SUB, g * own + m * SUB, SUB)
            if g > 0:
                put(0, g * own - HALO, HALO)
            if g < groups - 1:
                put(HALO + own, (g + 1) * own, HALO)
        if g == groups - 1:

            @pl.when(lat_ref[0] == bands - 1)
            def _():
                for f in (4, 5):
                    at = pl.ds(((HALO + own - 1) * 7 + f) * SUB, SUB)
                    piece_ref[g, at, :] = jnp.zeros((SUB, LANES), jnp.float32)

        first = 0 if g > 0 else HALO * 7 * SUB
        last = (height if g < groups - 1 else HALO + own) * 7 * SUB
        span = pl.ds(first, last - first)
        pltpu.make_async_copy(piece_ref.at[g, span], out_ref.at[g, span], sems.at[g]).start()
    for g in range(groups):
        first = 0 if g > 0 else HALO * 7 * SUB
        last = (height if g < groups - 1 else HALO + own) * 7 * SUB
        span = pl.ds(first, last - first)
        pltpu.make_async_copy(piece_ref.at[g, span], out_ref.at[g, span], sems.at[g]).wait()


def rim_kernel(south_ref, north_ref, packed_ref, out_ref, sems):
    groups, length = out_ref.shape[0], out_ref.shape[1]
    rim = HALO * 7 * SUB
    low = pltpu.make_async_copy(south_ref, out_ref.at[0, pl.ds(0, rim)], sems.at[0])
    high = pltpu.make_async_copy(north_ref, out_ref.at[groups - 1, pl.ds(length - rim, rim)], sems.at[1])
    low.start()
    high.start()
    low.wait()
    high.wait()


def unpack_kernel(in_ref, th_ref, wi_ref):
    groups = in_ref.shape[0]
    own = in_ref.shape[1] // (6 * SUB)
    for f in range(6):
        dst = th_ref.at[f] if f < 2 else wi_ref.at[f - 2]
        for g in range(groups):
            for m in range(own // SUB):
                for s in range(SUB):
                    dst[pl.ds(g * own + m * SUB, SUB), s * LANES : (s + 1) * LANES] = in_ref[
                        g, pl.ds((m * SUB * 6 + f) * SUB + s, SUB, stride=6 * SUB), :
                    ]


def step_kernel(
    merid_step,
    step_size,
    coef,
    flags,
    x_hbm,
    cut_ref,
    wfh_ref,
    wfl_ref,
    wbh_ref,
    wbl_ref,
    twc_ref,
    tws_ref,
    out_hbm,
    x_ref,
    s_ref,
    out_ref,
    t_ref,
    in_sems,
    out_sems,
    e_ref,
    z_ref,
    uu_ref,
    vv_ref,
    *y_refs,
):
    chunks = x_ref.shape[0]
    height = x_ref.shape[1] // 7
    own = height - 2 * HALO
    lane = lax.broadcasted_iota(jnp.int32, (SUB, LANES), 1)
    sub = lax.broadcasted_iota(jnp.int32, (SUB, LANES), 0)
    last_lane, first_lane = lane == LANES - 1, lane == 0
    last_sub, first_sub = sub == SUB - 1, sub == 0
    dy_inv = 1.0 / merid_step

    def east(xs):
        y = [pltpu.roll(x, LANES - 1, 1) for x in xs]
        r = [pltpu.roll(v, SUB - 1, 0) for v in y]
        return [
            jnp.where(last_lane, jnp.where(last_sub, r[(d + 1) % chunks], r[d]), y[d])
            for d in range(chunks)
        ]

    def west(xs):
        y = [pltpu.roll(x, 1, 1) for x in xs]
        r = [pltpu.roll(v, 1, 0) for v in y]
        return [
            jnp.where(first_lane, jnp.where(first_sub, r[d - 1], r[d]), y[d]) for d in range(chunks)
        ]

    cuts_in = (0, height // 3, 2 * height // 3, height)

    def arrival(i):
        rows = pl.ds(cuts_in[i] * 7, (cuts_in[i + 1] - cuts_in[i]) * 7)
        return pltpu.make_async_copy(x_hbm.at[:, rows], x_ref.at[:, rows], in_sems.at[i])

    def departure(i):
        rows = pl.ds(i * (own // 2) * 6, (own // 2) * 6)
        return pltpu.make_async_copy(out_ref.at[:, rows], out_hbm.at[:, rows], out_sems.at[i])

    for i in range(3):
        arrival(i).start()

    def stage(src, in_lo, fraction, final):
        fields = 7 if in_lo == 0 else 6
        in_hi = height - 1 - in_lo
        lo, hi = in_lo + 1, in_hi - 1
        count = hi - lo + 1

        def get(f, r):
            return [src[d, r * fields + f] for d in range(chunks)]

        def terrain(r):
            return [x_ref[d, r * 7 + 6] for d in range(chunks)]

        def corners(r, carry):
            rn = jnp.minimum(r + 1, in_hi)
            rs = jnp.maximum(r - 1, in_lo)
            c_half, cn_half = coef[0, r] * dy_inv, coef[0, rn] * dy_inv
            e_inv, sine = coef[2, r], coef[3, r]
            h0, h1, ground = get(0, r), get(1, r), terrain(r)
            base = [a + b for a, b in zip(h1, ground)]
            for k in range(2):
                u, v = get(2 + k, r), get(4 + k, r)
                uw, ve = west(u), east(v)
                un, vs = get(2 + k, rn), get(4 + k, rs)
                for d in range(chunks):
                    at = (r * 2 + k) * chunks + d
                    uu_ref[at] = u[d] + uw[d]
                    vv_ref[at] = v[d] + ve[d]
                    kin = 0.25 * (u[d] * u[d] + uw[d] * uw[d] + (v[d] * v[d] + vs[d] * vs[d]))
                    e_ref[at] = kin + (base[d] + (h0[d] if k == 0 else DENSITY_RATIO * h0[d]))
                    curl = (ve[d] - v[d]) - (un[d] * cn_half - u[d] * c_half)
                    z_ref[at] = sine + curl * e_inv
            return carry

        if in_lo == 0:
            for i in range(3):
                arrival(i).wait()
                first, last = cuts_in[i] - 1, cuts_in[i + 1] - 1
                lax.fori_loop(max(first, 0), height if i == 2 else last, corners, 0)
        else:
            lax.fori_loop(in_lo, in_hi + 1, corners, 0)

        def tendencies(r, carry):
            c_inv = coef[1, r]
            fn, fs = coef[4, r] * (0.5 * dy_inv), coef[4, r - 1] * (0.5 * dy_inv)
            live = coef[5, r]
            for k in range(2):

                def face(ref, row):
                    return [ref[(row * 2 + k) * chunks + d] for d in range(chunks)]

                def put(f, d, value):
                    start = (d * TILE_ROWS + (r - lo) * 6 + f) * SUB
                    t_ref[pl.ds(pl.multiple_of(start, SUB), SUB), :] = value

                h, hn, hs = get(k, r), get(k, r + 1), get(k, r - 1)
                u, v, vs = get(2 + k, r), get(4 + k, r), get(4 + k, r - 1)
                he = east(h)
                fx = [0.5 * (h[d] + he[d]) * u[d] for d in range(chunks)]
                fxw = west(fx)
                for d in range(chunks):
                    north = (h[d] + hn[d]) * (v[d] * fn) - (h[d] + hs[d]) * (vs[d] * fs)
                    put(k, d, ((fxw[d] - fx[d]) - north) * c_inv)
                z, zs, ec = face(z_ref, r), face(z_ref, r - 1), face(e_ref, r)
                vv, vvs = face(vv_ref, r), face(vv_ref, r - 1)
                ee = east(ec)
                for d in range(chunks):
                    turn = (0.125 * (z[d] + zs[d])) * (vv[d] + vvs[d])
                    put(2 + k, d, turn - (ee[d] - ec[d]) * c_inv)
                en, uu, uun = face(e_ref, r + 1), face(uu_ref, r), face(uu_ref, r + 1)
                zw = west(z)
                for d in range(chunks):
                    turn = (0.125 * (z[d] + zw[d])) * (uu[d] + uun[d])
                    put(4 + k, d, live * (dy_inv * (ec[d] - en[d]) - turn))
            return carry

        lax.fori_loop(lo, hi + 1, tendencies, 0)

        def circle_filter(p, carry):
            wave = lax.broadcasted_iota(jnp.int32, (PAIR, 2 * LANES), 1)
            wave = RADIX * jnp.where(wave >= LANES, wave - LANES, wave)

            def place(unit, a, half):
                d, s = a // SUB, a % SUB
                start = (d * TILE_ROWS + (p * UNITS + unit) * PAIR + half * SUB) * SUB + s
                return pl.ds(start, SUB, stride=SUB)

            def cut_of(unit):
                at = pl.multiple_of((p * UNITS + unit) * PAIR, PAIR)
                return cut_ref[in_lo, pl.ds(at, PAIR), :]

            def analyse(unit, half):
                re, im = real_fft([t_ref[place(unit, a, half), :] for a in range(RADIX)])
                for k in range(HALF + 1):
                    c, s = twc_ref[k : k + 1, :], tws_ref[k : k + 1, :]
                    if k == 0:
                        yr, yi = re[k], jnp.zeros_like(re[k])
                    elif im[k] is None:
                        yr, yi = re[k] * c, -(re[k] * s)
                    else:
                        yr, yi = re[k] * c + im[k] * s, im[k] * c - re[k] * s
                    at = pl.ds((k * 2 + half) * SUB, SUB)
                    y_refs[unit][at, 0:LANES] = yr
                    y_refs[unit][at, LANES : 2 * LANES] = yi

            def product(y, whi, wlo):
                n = y.shape[0]
                hi_part = y.astype(jnp.bfloat16)
                lo_part = (y - hi_part.astype(jnp.float32)).astype(jnp.bfloat16)
                dot = functools.partial(jnp.dot, preferred_element_type=jnp.float32)
                both = dot(jnp.concatenate([hi_part, lo_part], axis=0), whi)
                return both[:n] + both[n:] + dot(hi_part, wlo)

            def mask(unit, start):
                cut = cut_of(unit)
                cut2 = jnp.concatenate([cut, cut], axis=1)
                rows = slice(start * PAIR, (start + BLOCK) * PAIR)
                spec = product(y_refs[unit][rows, :], wfh_ref[...], wfl_ref[...])
                keep = []
                for k in range(start, start + BLOCK):
                    folded = jnp.minimum(wave + k, RADIX * LANES - k - wave)
                    keep.append(folded < cut2)
                spec = jnp.where(jnp.concatenate(keep, axis=0), spec, 0.0)
                y_refs[unit][rows, :] = product(spec, wbh_ref[...], wbl_ref[...])

            def synthesise(unit, half):
                re, im = [], []
                for k in range(HALF + 1):
                    c, s = twc_ref[k : k + 1, :], tws_ref[k : k + 1, :]
                    at = pl.ds((k * 2 + half) * SUB, SUB)
                    yr = y_refs[unit][at, 0:LANES]
                    if k == 0:
                        re.append(yr)
                        im.append(None)
                        continue
                    yi = y_refs[unit][at, LANES : 2 * LANES]
                    re.append(yr * c - yi * s)
                    im.append(None if k == HALF else yr * s + yi * c)
                circles = real_ifft(re, im)
                polar = cut_of(unit)[half * SUB : (half + 1) * SUB] < UNCUT
                for a in range(RADIX):
                    at = place(unit, a, half)
                    t_ref[at, :] = jnp.where(polar, circles[a], t_ref[at, :])

            for unit in range(UNITS):
                for half in range(2):
                    analyse(unit, half)
            for start in range(0, HALF + 1, BLOCK):
                for unit in range(UNITS):
                    mask(unit, start)
            for unit in range(UNITS):
                for half in range(2):
                    synthesise(unit, half)
            return carry

        @pl.when(flags[in_lo] > 0)
        def _():
            lax.fori_loop(0, -(-6 * count // (PAIR * UNITS)), circle_filter, 0)

        def update(r, carry):
            inside = coef[6, r]
            for f in range(6):
                for d in range(chunks):
                    start = (d * TILE_ROWS + (r - lo) * 6 + f) * SUB
                    change = t_ref[pl.ds(pl.multiple_of(start, SUB), SUB), :]
                    value = inside * (x_ref[d, r * 7 + f] + (fraction * step_size) * change)
                    if final:
                        out_ref[d, (r - HALO) * 6 + f] = value
                    else:
                        s_ref[d, r * 6 + f] = value
            return carry

        if final:
            for i in range(2):
                lax.fori_loop(lo + i * (own // 2), lo + (i + 1) * (own // 2), update, 0)
                departure(i).start()
            for i in range(2):
                departure(i).wait()
        else:
            lax.fori_loop(lo, hi + 1, update, 0)

    stage(x_ref, 0, 1.0 / 3.0, False)
    stage(s_ref, 1, 0.5, False)
    stage(s_ref, 2, 1.0, True)


def row_tables(cutoffs, row_start, height, total_rows, polar):
    row_ids = row_start - HALO + jnp.arange(height, dtype=jnp.int32)
    spacing = math.pi / total_rows
    centre_lat = -0.5 * math.pi + (row_ids.astype(jnp.float32) + 0.5) * spacing
    face_lat = -0.5 * math.pi + (row_ids.astype(jnp.float32) + 1.0) * spacing
    inside = jnp.where((row_ids >= 0) & (row_ids < total_rows), 1.0, 0.0).astype(jnp.float32)
    live = jnp.where((row_ids >= 0) & (row_ids < total_rows - 1), 1.0, 0.0).astype(jnp.float32)
    centre_cos = jnp.cos(centre_lat)
    face_cos = jnp.cos(face_lat) * live
    face_inverse = live / (face_cos + (1.0 - live))
    coef = jnp.stack(
        [centre_cos, 1.0 / centre_cos, face_inverse, jnp.sin(face_lat), face_cos, live, inside]
    )
    capped = ((row_ids >= 0) & (row_ids < polar)) | (
        (row_ids >= total_rows - polar) & (row_ids < total_rows)
    )
    position = jnp.where(row_ids < polar, row_ids, row_ids - (total_rows - 2 * polar))
    table_ids = jnp.arange(2 * polar, dtype=jnp.int32)
    cut = jnp.sum(
        jnp.where(position[:, None] == table_ids[None, :], cutoffs[None, :], 0), axis=1, dtype=jnp.int32
    )
    cut = jnp.where(capped, cut, UNCUT)
    stages = []
    for in_lo in range(3):
        rows = jnp.repeat(cut[in_lo + 1 : height - 1 - in_lo], 6)
        stages.append(jnp.pad(rows, (0, TILE_ROWS - rows.shape[0]), constant_values=UNCUT))
    cuts = jnp.stack(stages)
    flags = jnp.any(cuts < UNCUT, axis=1).astype(jnp.int32)
    return coef, flags, jnp.broadcast_to(cuts[:, :, None], (3, TILE_ROWS, LANES))


def body(thickness, winds, terrain, cutoffs):
    row_count, col_count = thickness.shape[1], thickness.shape[2]
    bands, sectors = lax.axis_size("lat"), lax.axis_size("lon")
    total_rows, circle = row_count * bands, col_count * sectors
    polar = (total_rows + 2) // 6
    own = row_count // sectors
    height = own + 2 * HALO
    merid_step = circle / (2.0 * total_rows)
    step_size = 0.1 * min(1.0, merid_step)
    lat = lax.axis_index("lat")
    flat = winds.reshape(4, row_count, col_count)

    vmem = pl.BlockSpec(memory_space=pltpu.VMEM)
    smem = pl.BlockSpec(memory_space=pltpu.SMEM)
    hbm = pl.BlockSpec(memory_space=pltpu.HBM)
    rim = jax.ShapeDtypeStruct((HALO * 7 * SUB, LANES), jnp.float32)
    tail, head = pl.pallas_call(
        edge_kernel,
        out_shape=(rim, rim),
        in_specs=[hbm] * 3,
        out_specs=(vmem, vmem),
        scratch_shapes=[
            pltpu.VMEM((2, 7, SUB, col_count), jnp.float32),
            pltpu.SemaphoreType.DMA((2, 7)),
        ],
        name="edge",
    )(thickness, flat, terrain)
    south = lax.ppermute(tail, "lat", [(i, i + 1) for i in range(bands - 1)])
    north = lax.ppermute(head, "lat", [(i + 1, i) for i in range(bands - 1)])

    piece = (sectors, height * 7 * SUB, LANES)
    packed = pl.pallas_call(
        functools.partial(pack_kernel, bands),
        out_shape=jax.ShapeDtypeStruct(piece, jnp.float32),
        in_specs=[smem] + [vmem] * 3,
        out_specs=hbm,
        scratch_shapes=[pltpu.VMEM(piece, jnp.float32), pltpu.SemaphoreType.DMA((sectors,))],
        compiler_params=pltpu.CompilerParams(vmem_limit_bytes=16 << 20),
        cost_estimate=pl.CostEstimate(flops=0, bytes_accessed=16 << 20, transcendentals=0),
        name="pack",
    )(lat.reshape(1).astype(jnp.int32), thickness, flat, terrain)
    packed = pl.pallas_call(
        rim_kernel,
        out_shape=jax.ShapeDtypeStruct(piece, jnp.float32),
        in_specs=[vmem, vmem, hbm],
        out_specs=hbm,
        scratch_shapes=[pltpu.SemaphoreType.DMA((2,))],
        input_output_aliases={2: 0},
        name="rim",
    )(south, north, packed)
    circles = lax.all_to_all(packed, "lon", 0, 0)

    row_start = lat * row_count + lax.axis_index("lon") * own
    coef, flags, cuts = row_tables(cutoffs, row_start, height, total_rows, polar)
    tables = [jnp.asarray(t) for t in filter_tables()]
    stepped = pl.pallas_call(
        functools.partial(step_kernel, merid_step, step_size),
        out_shape=jax.ShapeDtypeStruct((sectors, 6 * own, SUB, LANES), jnp.float32),
        in_specs=[smem, smem, hbm] + [vmem] * 7,
        out_specs=hbm,
        scratch_shapes=[
            pltpu.VMEM((sectors, 7 * height, SUB, LANES), jnp.float32),
            pltpu.VMEM((sectors, 6 * height, SUB, LANES), jnp.float32),
            pltpu.VMEM((sectors, 6 * own, SUB, LANES), jnp.float32),
            pltpu.VMEM((sectors * TILE_ROWS * SUB, LANES), jnp.float32),
            pltpu.SemaphoreType.DMA((3,)),
            pltpu.SemaphoreType.DMA((2,)),
        ]
        + [pltpu.VMEM((height * 2 * sectors, SUB, LANES), jnp.float32)] * 4
        + [pltpu.VMEM(((HALF + 1) * PAIR, 2 * LANES), jnp.float32)] * UNITS,
        compiler_params=pltpu.CompilerParams(vmem_limit_bytes=56 << 20),
        name="step",
    )(coef, flags, circles.reshape(sectors, 7 * height, SUB, LANES), cuts, *tables)
    returned = lax.all_to_all(stepped.reshape(sectors, 6 * own * SUB, LANES), "lon", 0, 0)
    new_thickness, new_winds = pl.pallas_call(
        unpack_kernel,
        out_shape=(
            jax.ShapeDtypeStruct(thickness.shape, jnp.float32),
            jax.ShapeDtypeStruct(flat.shape, jnp.float32),
        ),
        in_specs=[vmem],
        out_specs=(vmem, vmem),
        compiler_params=pltpu.CompilerParams(vmem_limit_bytes=40 << 20),
        name="unpack",
    )(returned)
    return new_thickness, new_winds.reshape(winds.shape)


def solution(mesh):
    in_specs = (P(None, "lat", "lon"), P(None, None, "lat", "lon"), P("lat", "lon"), P())
    out_specs = (P(None, "lat", "lon"), P(None, None, "lat", "lon"))
    return jax.shard_map(body, mesh=mesh, in_specs=in_specs, out_specs=out_specs, check_vma=False)
```

```python
import functools
import math

import jax
import jax.numpy as jnp
import ml_dtypes
import numpy as np
from jax import lax
from jax.experimental import pallas as pl
from jax.experimental.pallas import tpu as pltpu
from jax.sharding import PartitionSpec as P

DENSITY_RATIO = 0.9
HALO = 3
SUB = 8
LANES = 128
RADIX = 64
HALF = RADIX // 2
UNCUT = 1 << 20
TILE_ROWS = 64
PAIR = 16
UNITS = 3
BLOCK = 11
CUT = 12


def twisted(real, imag, k, n):
    angle = 2.0 * math.pi * k / n
    c, s = math.cos(angle), math.sin(angle)
    if k == 0:
        return real, imag
    if 8 * k == n:
        return (real + imag) * c, (imag - real) * c
    if 8 * k == 3 * n:
        return (imag - real) * s, -(real + imag) * s
    return real * c + imag * s, imag * c - real * s


def real_fft(x):
    n = len(x)
    if n == 1:
        return [x[0]], [None]
    er, ei = real_fft(x[0::2])
    odr, odi = real_fft(x[1::2])
    half = n // 2
    re, im = [None] * (half + 1), [None] * (half + 1)
    re[0], re[half] = er[0] + odr[0], er[0] - odr[0]
    for k in range(1, half // 2 + 1):
        if 2 * k == half:
            re[k], im[k] = er[k], -odr[k]
            continue
        tr, ti = twisted(odr[k], odi[k], k, n)
        re[k], im[k] = er[k] + tr, ei[k] + ti
        re[half - k], im[half - k] = er[k] - tr, ti - ei[k]
    return re, im


def real_ifft(re, im):
    n = 2 * (len(re) - 1)
    if n == 0:
        return [re[0]]
    half = n // 2
    if n == 2:
        return [re[0] + re[1], re[0] - re[1]]
    quarter = half // 2
    er, ei = [None] * (quarter + 1), [None] * (quarter + 1)
    odr, odi = [None] * (quarter + 1), [None] * (quarter + 1)
    er[0], odr[0] = re[0] + re[half], re[0] - re[half]
    for k in range(1, quarter + 1):
        if k == quarter:
            er[k], odr[k] = 2.0 * re[k], -2.0 * im[k]
            continue
        sr, si = re[k] + re[half - k], im[k] - im[half - k]
        dr, di = re[k] - re[half - k], im[k] + im[half - k]
        er[k], ei[k] = sr, si
        odi[k], odr[k] = twisted(di, dr, k, n)
    even = real_ifft(er, ei)
    odd = real_ifft(odr, odi)
    out = [None] * n
    out[0::2], out[1::2] = even, odd
    return out


def filter_tables():
    b = np.arange(LANES)
    angle = 2.0 * np.pi * (np.outer(b, b) % LANES) / LANES
    c, s = np.cos(angle), np.sin(angle)
    forward = np.block([[c, -s], [s, c]])
    backward = forward.T / (RADIX * LANES)

    def split(w):
        hi = w.astype(np.float32).astype(ml_dtypes.bfloat16)
        lo = (w - hi.astype(np.float64)).astype(np.float32).astype(ml_dtypes.bfloat16)
        return hi, lo

    k1 = np.arange(40)[:, None]
    twist = 2.0 * np.pi * k1 * b[None, :] / (RADIX * LANES)
    return (
        *split(forward),
        *split(backward),
        np.cos(twist).astype(np.float32),
        np.sin(twist).astype(np.float32),
    )


def edge_kernel(th_ref, wi_ref, te_ref, tail_ref, head_ref, tile_ref, sems):
    rows = te_ref.shape[0]

    def copies(f):
        src = th_ref.at[f] if f < 2 else wi_ref.at[f - 2] if f < 6 else te_ref
        return [
            pltpu.make_async_copy(src.at[pl.ds(start, SUB)], tile_ref.at[i, f], sems.at[i, f])
            for i, start in enumerate((rows - SUB, 0))
        ]

    for f in range(7):
        for copy in copies(f):
            copy.start()
    for f in range(7):
        for i, copy in enumerate(copies(f)):
            copy.wait()
            out_ref, start = ((tail_ref, SUB - HALO), (head_ref, 0))[i]
            for s in range(SUB):
                out_ref[pl.ds(f * SUB + s, HALO, stride=7 * SUB), :] = tile_ref[
                    i, f, start : start + HALO, s * LANES : (s + 1) * LANES
                ]


def pack_kernel(bands, lat_ref, th_ref, wi_ref, te_ref, a_hbm, b_hbm, piece_ref, sems):
    groups = piece_ref.shape[0]
    height = piece_ref.shape[1] // (7 * SUB)
    own = height - 2 * HALO
    split = CUT * 7 * SUB

    def departures(g):
        a_first = 0 if g > 0 else HALO * 7 * SUB
        b_last = (height if g < groups - 1 else HALO + own) * 7 * SUB
        a, b = pl.ds(a_first, split - a_first), pl.ds(split, b_last - split)
        return (
            pltpu.make_async_copy(piece_ref.at[g, a], a_hbm.at[g, a], sems.at[0, g]),
            pltpu.make_async_copy(piece_ref.at[g, b], b_hbm.at[g, pl.ds(0, b_last - split)], sems.at[1, g]),
        )

    for g in range(groups):
        for f in range(7):
            src = th_ref.at[f] if f < 2 else wi_ref.at[f - 2] if f < 6 else te_ref

            def put(dst, start, count):
                for s in range(SUB):
                    piece_ref[g, pl.ds((dst * 7 + f) * SUB + s, count, stride=7 * SUB), :] = src[
                        pl.ds(start, count), s * LANES : (s + 1) * LANES
                    ]

            for m in range(own // SUB):
                put(HALO + m * SUB, g * own + m * SUB, SUB)
            if g > 0:
                put(0, g * own - HALO, HALO)
            if g < groups - 1:
                put(HALO + own, (g + 1) * own, HALO)
        if g == groups - 1:

            @pl.when(lat_ref[0] == bands - 1)
            def _():
                for f in (4, 5):
                    at = pl.ds(((HALO + own - 1) * 7 + f) * SUB, SUB)
                    piece_ref[g, at, :] = jnp.zeros((SUB, LANES), jnp.float32)

        for copy in departures(g):
            copy.start()
    for g in range(groups):
        for copy in departures(g):
            copy.wait()


def rim_kernel(group, start, rim_ref, packed_ref, out_ref, sem):
    copy = pltpu.make_async_copy(rim_ref, out_ref.at[group, pl.ds(start, rim_ref.shape[0])], sem)
    copy.start()
    copy.wait()


def unpack_kernel(a_ref, b_ref, th_ref, wi_ref):
    groups = a_ref.shape[0]
    spans = [(r.shape[1] // (6 * SUB), r) for r in (a_ref, b_ref)]
    own = spans[0][0] + spans[1][0]
    for f in range(6):
        dst = th_ref.at[f] if f < 2 else wi_ref.at[f - 2]
        for g in range(groups):
            row = g * own
            for rows, src in spans:
                for first in range(0, rows, SUB):
                    count = min(SUB, rows - first)
                    for s in range(SUB):
                        dst[pl.ds(row + first, count), s * LANES : (s + 1) * LANES] = src[
                            g, pl.ds((first * 6 + f) * SUB + s, count, stride=6 * SUB), :
                        ]
                row += rows


def stage_rows(height, upper):
    if upper:
        return [(CUT - 1 - k, height - 2 - k) for k in range(3)]
    return [(1 + k, CUT - 2 - k) for k in range(3)]


def step_kernel(upper, height, merid_step, step_size, coef, flags, *refs):
    if upper:
        x_low, x_high, s1_hbm, s2_hbm, *refs = refs
    else:
        x_low, *refs = refs
    cut_ref, wfh_ref, wfl_ref, wbh_ref, wbl_ref, twc_ref, tws_ref, *refs = refs
    out_hbm, *refs = refs
    if not upper:
        s1_hbm, s2_hbm, *refs = refs
    x_ref, s1_ref, s2_ref, out_ref, t_ref, in_sems, out_sems, edge_sems, *refs = refs
    e_ref, z_ref, uu_ref, vv_ref, *y_refs = refs
    chunks = x_ref.shape[0]
    ranges = stage_rows(height, upper)
    out_lo, out_hi = ranges[2]
    out_rows = out_hi - out_lo + 1
    lane = lax.broadcasted_iota(jnp.int32, (SUB, LANES), 1)
    sub = lax.broadcasted_iota(jnp.int32, (SUB, LANES), 0)
    last_lane, first_lane = lane == LANES - 1, lane == 0
    last_sub, first_sub = sub == SUB - 1, sub == 0
    dy_inv = 1.0 / merid_step

    def east(xs):
        y = [pltpu.roll(x, LANES - 1, 1) for x in xs]
        r = [pltpu.roll(v, SUB - 1, 0) for v in y]
        return [
            jnp.where(last_lane, jnp.where(last_sub, r[(d + 1) % chunks], r[d]), y[d])
            for d in range(chunks)
        ]

    def west(xs):
        y = [pltpu.roll(x, 1, 1) for x in xs]
        r = [pltpu.roll(v, 1, 0) for v in y]
        return [
            jnp.where(first_lane, jnp.where(first_sub, r[d - 1], r[d]), y[d]) for d in range(chunks)
        ]

    def x_copy(i, src, src_row, row, count):
        return pltpu.make_async_copy(
            src.at[:, pl.ds(src_row * 7, count * 7)], x_ref.at[:, pl.ds(row * 7, count * 7)], in_sems.at[i]
        )

    if upper:
        half = (height - CUT) // 2
        arrivals = [
            x_copy(0, x_low, CUT - HALO, CUT - HALO, HALO),
            x_copy(1, x_high, 0, CUT, half),
            x_copy(2, x_high, half, CUT + half, height - CUT - half),
        ]
        in_edges = (CUT, CUT + half, height)
    else:
        arrivals = [x_copy(i, x_low, i * CUT // 3, i * CUT // 3, CUT // 3) for i in range(3)]
        in_edges = tuple((i + 1) * CUT // 3 for i in range(3))

    def departure(i):
        rows = pl.ds(i * (out_rows // 2) * 6, (out_rows // 2) * 6)
        return pltpu.make_async_copy(out_ref.at[:, rows], out_hbm.at[:, rows], out_sems.at[i])

    def edge(i):
        hbm, ref = ((s1_hbm, s1_ref), (s2_hbm, s2_ref))[i]
        ref = ref.at[:, pl.ds((CUT - 3 - i) * 6, 12)]
        src, dst = (hbm, ref) if upper else (ref, hbm)
        return pltpu.make_async_copy(src, dst, edge_sems.at[i])

    for copy in arrivals:
        copy.start()
    if upper:
        edge(0).start()
        edge(1).start()

    def stage(src, dst, index, fraction):
        fields = 7 if index == 0 else 6
        final = index == 2
        lo, hi = ranges[index]
        in_lo, in_hi = lo - 1, hi + 1
        count = hi - lo + 1

        def get(f, r):
            return [src[d, r * fields + f] for d in range(chunks)]

        def terrain(r):
            return [x_ref[d, r * 7 + 6] for d in range(chunks)]

        def corners(r, carry):
            rn = jnp.minimum(r + 1, in_hi)
            rs = jnp.maximum(r - 1, in_lo)
            c_half, cn_half = coef[0, r] * dy_inv, coef[0, rn] * dy_inv
            e_inv, sine = coef[2, r], coef[3, r]
            h0, h1, ground = get(0, r), get(1, r), terrain(r)
            base = [a + b for a, b in zip(h1, ground)]
            for k in range(2):
                u, v = get(2 + k, r), get(4 + k, r)
                uw, ve = west(u), east(v)
                un, vs = get(2 + k, rn), get(4 + k, rs)
                for d in range(chunks):
                    at = (r * 2 + k) * chunks + d
                    uu_ref[at] = u[d] + uw[d]
                    vv_ref[at] = v[d] + ve[d]
                    kin = 0.25 * (u[d] * u[d] + uw[d] * uw[d] + (v[d] * v[d] + vs[d] * vs[d]))
                    e_ref[at] = kin + (base[d] + (h0[d] if k == 0 else DENSITY_RATIO * h0[d]))
                    curl = (ve[d] - v[d]) - (un[d] * cn_half - u[d] * c_half)
                    z_ref[at] = sine + curl * e_inv
            return carry

        if index == 0:
            first = in_lo
            for i in range(3):
                arrivals[i].wait()
                last = in_edges[i] - 1 if i < 2 else in_edges[i]
                lax.fori_loop(first, last, corners, 0)
                first = last
        else:
            if upper:
                edge(index - 1).wait()
            lax.fori_loop(in_lo, in_hi + 1, corners, 0)

        def tendencies(r, carry):
            c_inv = coef[1, r]
            fn, fs = coef[4, r] * (0.5 * dy_inv), coef[4, r - 1] * (0.5 * dy_inv)
            live = coef[5, r]
            for k in range(2):

                def face(ref, row):
                    return [ref[(row * 2 + k) * chunks + d] for d in range(chunks)]

                def put(f, d, value):
                    start = (d * TILE_ROWS + (r - lo) * 6 + f) * SUB
                    t_ref[pl.ds(pl.multiple_of(start, SUB), SUB), :] = value

                h, hn, hs = get(k, r), get(k, r + 1), get(k, r - 1)
                u, v, vs = get(2 + k, r), get(4 + k, r), get(4 + k, r - 1)
                he = east(h)
                fx = [0.5 * (h[d] + he[d]) * u[d] for d in range(chunks)]
                fxw = west(fx)
                for d in range(chunks):
                    north = (h[d] + hn[d]) * (v[d] * fn) - (h[d] + hs[d]) * (vs[d] * fs)
                    put(k, d, ((fxw[d] - fx[d]) - north) * c_inv)
                z, zs, ec = face(z_ref, r), face(z_ref, r - 1), face(e_ref, r)
                vv, vvs = face(vv_ref, r), face(vv_ref, r - 1)
                ee = east(ec)
                for d in range(chunks):
                    turn = (0.125 * (z[d] + zs[d])) * (vv[d] + vvs[d])
                    put(2 + k, d, turn - (ee[d] - ec[d]) * c_inv)
                en, uu, uun = face(e_ref, r + 1), face(uu_ref, r), face(uu_ref, r + 1)
                zw = west(z)
                for d in range(chunks):
                    turn = (0.125 * (z[d] + zw[d])) * (uu[d] + uun[d])
                    put(4 + k, d, live * (dy_inv * (ec[d] - en[d]) - turn))
            return carry

        lax.fori_loop(lo, hi + 1, tendencies, 0)

        total = -(-6 * count // PAIR)
        units = 3 if total % 3 == 0 else 2

        def circle_filter(p, carry):
            wave = lax.broadcasted_iota(jnp.int32, (PAIR, 2 * LANES), 1)
            wave = RADIX * jnp.where(wave >= LANES, wave - LANES, wave)

            def place(unit, a, half):
                d, s = a // SUB, a % SUB
                start = (d * TILE_ROWS + (p * units + unit) * PAIR + half * SUB) * SUB + s
                return pl.ds(start, SUB, stride=SUB)

            def cut_of(unit):
                at = pl.multiple_of((p * units + unit) * PAIR, PAIR)
                return cut_ref[index, pl.ds(at, PAIR), :]

            def analyse(unit, half):
                re, im = real_fft([t_ref[place(unit, a, half), :] for a in range(RADIX)])
                for k in range(HALF + 1):
                    c, s = twc_ref[k : k + 1, :], tws_ref[k : k + 1, :]
                    if k == 0:
                        yr, yi = re[k], jnp.zeros_like(re[k])
                    elif im[k] is None:
                        yr, yi = re[k] * c, -(re[k] * s)
                    else:
                        yr, yi = re[k] * c + im[k] * s, im[k] * c - re[k] * s
                    at = pl.ds((k * 2 + half) * SUB, SUB)
                    y_refs[unit][at, 0:LANES] = yr
                    y_refs[unit][at, LANES : 2 * LANES] = yi

            def product(y, whi, wlo):
                n = y.shape[0]
                hi_part = y.astype(jnp.bfloat16)
                lo_part = (y - hi_part.astype(jnp.float32)).astype(jnp.bfloat16)
                dot = functools.partial(jnp.dot, preferred_element_type=jnp.float32)
                both = dot(jnp.concatenate([hi_part, lo_part], axis=0), whi)
                return both[:n] + both[n:] + dot(hi_part, wlo)

            def mask(unit, start):
                cut = cut_of(unit)
                cut2 = jnp.concatenate([cut, cut], axis=1)
                rows = slice(start * PAIR, (start + BLOCK) * PAIR)
                spec = product(y_refs[unit][rows, :], wfh_ref[...], wfl_ref[...])
                keep = []
                for k in range(start, start + BLOCK):
                    folded = jnp.minimum(wave + k, RADIX * LANES - k - wave)
                    keep.append(folded < cut2)
                spec = jnp.where(jnp.concatenate(keep, axis=0), spec, 0.0)
                y_refs[unit][rows, :] = product(spec, wbh_ref[...], wbl_ref[...])

            def synthesise(unit, half):
                re, im = [], []
                for k in range(HALF + 1):
                    c, s = twc_ref[k : k + 1, :], tws_ref[k : k + 1, :]
                    at = pl.ds((k * 2 + half) * SUB, SUB)
                    yr = y_refs[unit][at, 0:LANES]
                    if k == 0:
                        re.append(yr)
                        im.append(None)
                        continue
                    yi = y_refs[unit][at, LANES : 2 * LANES]
                    re.append(yr * c - yi * s)
                    im.append(None if k == HALF else yr * s + yi * c)
                circles = real_ifft(re, im)
                polar = cut_of(unit)[half * SUB : (half + 1) * SUB] < UNCUT
                for a in range(RADIX):
                    at = place(unit, a, half)
                    t_ref[at, :] = jnp.where(polar, circles[a], t_ref[at, :])

            for unit in range(units):
                for half in range(2):
                    analyse(unit, half)
            for start in range(0, HALF + 1, BLOCK):
                for unit in range(units):
                    mask(unit, start)
            for unit in range(units):
                for half in range(2):
                    synthesise(unit, half)
            return carry

        @pl.when(flags[index] > 0)
        def _():
            lax.fori_loop(0, -(-total // units), circle_filter, 0)

        def update(r, carry):
            inside = coef[6, r]
            for f in range(6):
                for d in range(chunks):
                    start = (d * TILE_ROWS + (r - lo) * 6 + f) * SUB
                    change = t_ref[pl.ds(pl.multiple_of(start, SUB), SUB), :]
                    value = inside * (x_ref[d, r * 7 + f] + (fraction * step_size) * change)
                    if final:
                        out_ref[d, (r - lo) * 6 + f] = value
                    else:
                        dst[d, r * 6 + f] = value
            return carry

        if final:
            for i in range(2):
                lax.fori_loop(lo + i * (count // 2), lo + (i + 1) * (count // 2), update, 0)
                departure(i).start()
        else:
            lax.fori_loop(lo, hi + 1, update, 0)
            if not upper:
                edge(index).start()

    stage(x_ref, s1_ref, 0, 1.0 / 3.0)
    stage(s1_ref, s2_ref, 1, 0.5)
    stage(s2_ref, None, 2, 1.0)
    for i in range(2):
        departure(i).wait()
        if not upper:
            edge(i).wait()


def row_tables(cutoffs, row_start, height, total_rows, polar):
    row_ids = row_start - HALO + jnp.arange(height, dtype=jnp.int32)
    spacing = math.pi / total_rows
    centre_lat = -0.5 * math.pi + (row_ids.astype(jnp.float32) + 0.5) * spacing
    face_lat = -0.5 * math.pi + (row_ids.astype(jnp.float32) + 1.0) * spacing
    inside = jnp.where((row_ids >= 0) & (row_ids < total_rows), 1.0, 0.0).astype(jnp.float32)
    live = jnp.where((row_ids >= 0) & (row_ids < total_rows - 1), 1.0, 0.0).astype(jnp.float32)
    centre_cos = jnp.cos(centre_lat)
    face_cos = jnp.cos(face_lat) * live
    face_inverse = live / (face_cos + (1.0 - live))
    coef = jnp.stack(
        [centre_cos, 1.0 / centre_cos, face_inverse, jnp.sin(face_lat), face_cos, live, inside]
    )
    capped = ((row_ids >= 0) & (row_ids < polar)) | (
        (row_ids >= total_rows - polar) & (row_ids < total_rows)
    )
    position = jnp.where(row_ids < polar, row_ids, row_ids - (total_rows - 2 * polar))
    table_ids = jnp.arange(2 * polar, dtype=jnp.int32)
    cut = jnp.sum(
        jnp.where(position[:, None] == table_ids[None, :], cutoffs[None, :], 0), axis=1, dtype=jnp.int32
    )
    cut = jnp.where(capped, cut, UNCUT)
    parts = []
    for upper in (False, True):
        stages = []
        for lo, hi in stage_rows(height, upper):
            rows = jnp.repeat(cut[lo : hi + 1], 6)
            stages.append(jnp.pad(rows, (0, TILE_ROWS - rows.shape[0]), constant_values=UNCUT))
        cuts = jnp.stack(stages)
        flags = jnp.any(cuts < UNCUT, axis=1).astype(jnp.int32)
        parts.append((flags, jnp.broadcast_to(cuts[:, :, None], (3, TILE_ROWS, LANES))))
    return coef, parts


def body(thickness, winds, terrain, cutoffs):
    row_count, col_count = thickness.shape[1], thickness.shape[2]
    bands, sectors = lax.axis_size("lat"), lax.axis_size("lon")
    total_rows, circle = row_count * bands, col_count * sectors
    polar = (total_rows + 2) // 6
    own = row_count // sectors
    height = own + 2 * HALO
    merid_step = circle / (2.0 * total_rows)
    step_size = 0.1 * min(1.0, merid_step)
    lat = lax.axis_index("lat")
    flat = winds.reshape(4, row_count, col_count)

    vmem = pl.BlockSpec(memory_space=pltpu.VMEM)
    smem = pl.BlockSpec(memory_space=pltpu.SMEM)
    hbm = pl.BlockSpec(memory_space=pltpu.HBM)
    rim = jax.ShapeDtypeStruct((HALO * 7 * SUB, LANES), jnp.float32)
    tail, head = pl.pallas_call(
        edge_kernel,
        out_shape=(rim, rim),
        in_specs=[hbm] * 3,
        out_specs=(vmem, vmem),
        scratch_shapes=[
            pltpu.VMEM((2, 7, SUB, col_count), jnp.float32),
            pltpu.SemaphoreType.DMA((2, 7)),
        ],
        name="edge",
    )(thickness, flat, terrain)
    south = lax.ppermute(tail, "lat", [(i, i + 1) for i in range(bands - 1)])
    north = lax.ppermute(head, "lat", [(i + 1, i) for i in range(bands - 1)])

    def piece(rows, fields):
        return jax.ShapeDtypeStruct((sectors, rows * fields * SUB, LANES), jnp.float32)

    packed_low, packed_high = pl.pallas_call(
        functools.partial(pack_kernel, bands),
        out_shape=(piece(CUT, 7), piece(height - CUT, 7)),
        in_specs=[smem] + [vmem] * 3,
        out_specs=(hbm, hbm),
        scratch_shapes=[
            pltpu.VMEM(piece(height, 7).shape, jnp.float32),
            pltpu.SemaphoreType.DMA((2, sectors)),
        ],
        compiler_params=pltpu.CompilerParams(vmem_limit_bytes=56 << 20),
        cost_estimate=pl.CostEstimate(flops=0, bytes_accessed=12 << 20, transcendentals=0),
        name="pack",
    )(lat.reshape(1).astype(jnp.int32), thickness, flat, terrain)

    def rimmed(packed, rows, group, start):
        return pl.pallas_call(
            functools.partial(rim_kernel, group, start),
            out_shape=jax.ShapeDtypeStruct(packed.shape, jnp.float32),
            in_specs=[vmem, hbm],
            out_specs=hbm,
            scratch_shapes=[pltpu.SemaphoreType.DMA],
            input_output_aliases={1: 0},
            name="rim",
        )(rows, packed)

    packed_low = rimmed(packed_low, south, 0, 0)
    packed_high = rimmed(packed_high, north, sectors - 1, (HALO + own - CUT) * 7 * SUB)
    circles_low = lax.all_to_all(packed_low, "lon", 0, 0)
    circles_high = lax.all_to_all(packed_high, "lon", 0, 0)

    row_start = lat * row_count + lax.axis_index("lon") * own
    coef, parts = row_tables(cutoffs, row_start, height, total_rows, polar)
    tables = [jnp.asarray(t) for t in filter_tables()]
    edges = jax.ShapeDtypeStruct((sectors, 12, SUB, LANES), jnp.float32)

    def step(upper, states, saved):
        lo, hi = stage_rows(height, upper)[2]
        out = jax.ShapeDtypeStruct((sectors, 6 * (hi - lo + 1), SUB, LANES), jnp.float32)
        flags, cuts = parts[upper]
        states = [x.reshape(sectors, -1, SUB, LANES) for x in states]
        return pl.pallas_call(
            functools.partial(step_kernel, upper, height, merid_step, step_size),
            out_shape=out if upper else (out, edges, edges),
            in_specs=[smem, smem] + [hbm] * len(states + saved) + [vmem] * 7,
            out_specs=hbm if upper else (hbm, hbm, hbm),
            scratch_shapes=[
                pltpu.VMEM((sectors, 7 * height, SUB, LANES), jnp.float32),
                pltpu.VMEM((sectors, 6 * height, SUB, LANES), jnp.float32),
                pltpu.VMEM((sectors, 6 * height, SUB, LANES), jnp.float32),
                pltpu.VMEM(out.shape, jnp.float32),
                pltpu.VMEM((sectors * TILE_ROWS * SUB, LANES), jnp.float32),
                pltpu.SemaphoreType.DMA((3,)),
                pltpu.SemaphoreType.DMA((2,)),
                pltpu.SemaphoreType.DMA((2,)),
            ]
            + [pltpu.VMEM((height * 2 * sectors, SUB, LANES), jnp.float32)] * 4
            + [pltpu.VMEM(((HALF + 1) * PAIR, 2 * LANES), jnp.float32)] * UNITS,
            compiler_params=pltpu.CompilerParams(vmem_limit_bytes=57 << 20),
            cost_estimate=pl.CostEstimate(flops=0, bytes_accessed=64 << 20, transcendentals=0),
            name="step_high" if upper else "step_low",
        )(coef, flags, *states, *saved, cuts, *tables)

    new_low, *saved = step(False, [circles_low], [])
    returned_low = lax.all_to_all(new_low.reshape(sectors, -1, LANES), "lon", 0, 0)
    new_high = step(True, [circles_low, circles_high], saved)
    returned_high = lax.all_to_all(new_high.reshape(sectors, -1, LANES), "lon", 0, 0)
    new_thickness, new_winds = pl.pallas_call(
        unpack_kernel,
        out_shape=(
            jax.ShapeDtypeStruct(thickness.shape, jnp.float32),
            jax.ShapeDtypeStruct(flat.shape, jnp.float32),
        ),
        in_specs=[vmem, vmem],
        out_specs=(vmem, vmem),
        compiler_params=pltpu.CompilerParams(vmem_limit_bytes=40 << 20),
        name="unpack",
    )(returned_low, returned_high)
    return new_thickness, new_winds.reshape(winds.shape)


def solution(mesh):
    in_specs = (P(None, "lat", "lon"), P(None, None, "lat", "lon"), P("lat", "lon"), P())
    out_specs = (P(None, "lat", "lon"), P(None, None, "lat", "lon"))
    return jax.shard_map(body, mesh=mesh, in_specs=in_specs, out_specs=out_specs, check_vma=False)
```

```python
import functools
import math

import jax
import jax.numpy as jnp
import ml_dtypes
import numpy as np
from jax import lax
from jax.experimental import pallas as pl
from jax.experimental.pallas import tpu as pltpu
from jax.sharding import PartitionSpec as P

DENSITY_RATIO = 0.9
HALO = 3
SUB = 8
LANES = 128
RADIX = 64
HALF = RADIX // 2
UNCUT = 1 << 20
TILE_ROWS = 96
PAIR = 16
UNITS = 3
BLOCK = 11
CUT = 14


def twisted(real, imag, k, n):
    angle = 2.0 * math.pi * k / n
    c, s = math.cos(angle), math.sin(angle)
    if k == 0:
        return real, imag
    if 8 * k == n:
        return (real + imag) * c, (imag - real) * c
    if 8 * k == 3 * n:
        return (imag - real) * s, -(real + imag) * s
    return real * c + imag * s, imag * c - real * s


def real_fft(x):
    n = len(x)
    if n == 1:
        return [x[0]], [None]
    er, ei = real_fft(x[0::2])
    odr, odi = real_fft(x[1::2])
    half = n // 2
    re, im = [None] * (half + 1), [None] * (half + 1)
    re[0], re[half] = er[0] + odr[0], er[0] - odr[0]
    for k in range(1, half // 2 + 1):
        if 2 * k == half:
            re[k], im[k] = er[k], -odr[k]
            continue
        tr, ti = twisted(odr[k], odi[k], k, n)
        re[k], im[k] = er[k] + tr, ei[k] + ti
        re[half - k], im[half - k] = er[k] - tr, ti - ei[k]
    return re, im


def real_ifft(re, im):
    n = 2 * (len(re) - 1)
    if n == 0:
        return [re[0]]
    half = n // 2
    if n == 2:
        return [re[0] + re[1], re[0] - re[1]]
    quarter = half // 2
    er, ei = [None] * (quarter + 1), [None] * (quarter + 1)
    odr, odi = [None] * (quarter + 1), [None] * (quarter + 1)
    er[0], odr[0] = re[0] + re[half], re[0] - re[half]
    for k in range(1, quarter + 1):
        if k == quarter:
            er[k], odr[k] = 2.0 * re[k], -2.0 * im[k]
            continue
        sr, si = re[k] + re[half - k], im[k] - im[half - k]
        dr, di = re[k] - re[half - k], im[k] + im[half - k]
        er[k], ei[k] = sr, si
        odi[k], odr[k] = twisted(di, dr, k, n)
    even = real_ifft(er, ei)
    odd = real_ifft(odr, odi)
    out = [None] * n
    out[0::2], out[1::2] = even, odd
    return out


def filter_tables():
    b = np.arange(LANES)
    angle = 2.0 * np.pi * (np.outer(b, b) % LANES) / LANES
    c, s = np.cos(angle), np.sin(angle)
    forward = np.block([[c, -s], [s, c]])
    backward = forward.T / (RADIX * LANES)

    def split(w):
        hi = w.astype(np.float32).astype(ml_dtypes.bfloat16)
        lo = (w - hi.astype(np.float64)).astype(np.float32).astype(ml_dtypes.bfloat16)
        return hi, lo

    k1 = np.arange(40)[:, None]
    twist = 2.0 * np.pi * k1 * b[None, :] / (RADIX * LANES)
    return (
        *split(forward),
        *split(backward),
        np.cos(twist).astype(np.float32),
        np.sin(twist).astype(np.float32),
    )


def edge_kernel(th_ref, wi_ref, te_ref, tail_ref, head_ref, tile_ref, sems):
    rows = te_ref.shape[0]

    def copies(f):
        src = th_ref.at[f] if f < 2 else wi_ref.at[f - 2] if f < 6 else te_ref
        return [
            pltpu.make_async_copy(src.at[pl.ds(start, SUB)], tile_ref.at[i, f], sems.at[i, f])
            for i, start in enumerate((rows - SUB, 0))
        ]

    for f in range(7):
        for copy in copies(f):
            copy.start()
    for f in range(7):
        for i, copy in enumerate(copies(f)):
            copy.wait()
            out_ref, start = ((tail_ref, SUB - HALO), (head_ref, 0))[i]
            for s in range(SUB):
                out_ref[pl.ds(f * SUB + s, HALO, stride=7 * SUB), :] = tile_ref[
                    i, f, start : start + HALO, s * LANES : (s + 1) * LANES
                ]


def pack_kernel(bands, lat_ref, th_hbm, wi_hbm, te_hbm, a_hbm, b_hbm, th_ref, wi_ref, te_ref, piece_ref, in_sems, sems):
    groups = piece_ref.shape[0]
    height = piece_ref.shape[1] // (7 * SUB)
    own = height - 2 * HALO
    split = CUT * 7 * SUB

    def arrivals(g):
        rows = pl.ds(g * own, own)
        return (
            pltpu.make_async_copy(th_hbm.at[:, rows], th_ref.at[:, rows], in_sems.at[0, g]),
            pltpu.make_async_copy(wi_hbm.at[:, rows], wi_ref.at[:, rows], in_sems.at[1, g]),
            pltpu.make_async_copy(te_hbm.at[rows], te_ref.at[rows], in_sems.at[2, g]),
        )

    def departures(g):
        a_first = 0 if g > 0 else HALO * 7 * SUB
        b_last = (height if g < groups - 1 else HALO + own) * 7 * SUB
        a, b = pl.ds(a_first, split - a_first), pl.ds(split, b_last - split)
        return (
            pltpu.make_async_copy(piece_ref.at[g, a], a_hbm.at[g, a], sems.at[0, g]),
            pltpu.make_async_copy(piece_ref.at[g, b], b_hbm.at[g, pl.ds(0, b_last - split)], sems.at[1, g]),
        )

    for g in range(groups):
        for copy in arrivals(g):
            copy.start()
    for copy in arrivals(0):
        copy.wait()
    for g in range(groups):
        if g < groups - 1:
            for copy in arrivals(g + 1):
                copy.wait()
        for f in range(7):
            src = th_ref.at[f] if f < 2 else wi_ref.at[f - 2] if f < 6 else te_ref

            def put(dst, start, count):
                for s in range(SUB):
                    piece_ref[g, pl.ds((dst * 7 + f) * SUB + s, count, stride=7 * SUB), :] = src[
                        pl.ds(start, count), s * LANES : (s + 1) * LANES
                    ]

            for m in range(own // SUB):
                put(HALO + m * SUB, g * own + m * SUB, SUB)
            if g > 0:
                put(0, g * own - HALO, HALO)
            if g < groups - 1:
                put(HALO + own, (g + 1) * own, HALO)
        if g == groups - 1:

            @pl.when(lat_ref[0] == bands - 1)
            def _():
                for f in (4, 5):
                    at = pl.ds(((HALO + own - 1) * 7 + f) * SUB, SUB)
                    piece_ref[g, at, :] = jnp.zeros((SUB, LANES), jnp.float32)

        for copy in departures(g):
            copy.start()
    for g in range(groups):
        for copy in departures(g):
            copy.wait()


def rim_kernel(group, start, rim_ref, packed_ref, out_ref, sem):
    copy = pltpu.make_async_copy(rim_ref, out_ref.at[group, pl.ds(start, rim_ref.shape[0])], sem)
    copy.start()
    copy.wait()


def unpack_kernel(first, *refs):
    in_ref, th_hbm, wi_hbm, tile_ref, sems = refs if first == 0 else (refs[0], *refs[3:])
    groups = in_ref.shape[0]
    rows = in_ref.shape[1] // (6 * SUB)

    def departure(f, g):
        dst = th_hbm.at[f] if f < 2 else wi_hbm.at[f - 2]
        block = pl.ds(g * 2 * rows + first, rows)
        return pltpu.make_async_copy(tile_ref.at[f, g], dst.at[block], sems.at[f, g])

    for f in range(6):
        for g in range(groups):
            for s in range(SUB):
                tile_ref[f, g, :, s * LANES : (s + 1) * LANES] = in_ref[
                    g, pl.ds(f * SUB + s, rows, stride=6 * SUB), :
                ]
            departure(f, g).start()
    for f in range(6):
        for g in range(groups):
            departure(f, g).wait()


def stage_rows(height, upper):
    if upper:
        return [(CUT - 1 - k, height - 2 - k) for k in range(3)]
    return [(1 + k, CUT - 2 - k) for k in range(3)]


def step_kernel(upper, height, merid_step, step_size, coef, flags, *refs):
    if upper:
        x_low, x_high, s1_hbm, s2_hbm, *refs = refs
    else:
        x_low, *refs = refs
    cut_ref, wfh_ref, wfl_ref, wbh_ref, wbl_ref, twc_ref, tws_ref, *refs = refs
    out_hbm, *refs = refs
    if not upper:
        s1_hbm, s2_hbm, *refs = refs
    x_ref, s1_ref, s2_ref, out_ref, t_ref, in_sems, out_sems, edge_sems, *refs = refs
    e_ref, z_ref, uu_ref, vv_ref, *y_refs = refs
    chunks = x_ref.shape[0]
    ranges = stage_rows(height, upper)
    out_lo, out_hi = ranges[2]
    out_rows = out_hi - out_lo + 1
    lane = lax.broadcasted_iota(jnp.int32, (SUB, LANES), 1)
    sub = lax.broadcasted_iota(jnp.int32, (SUB, LANES), 0)
    last_lane, first_lane = lane == LANES - 1, lane == 0
    last_sub, first_sub = sub == SUB - 1, sub == 0
    dy_inv = 1.0 / merid_step

    def east(xs):
        y = [pltpu.roll(x, LANES - 1, 1) for x in xs]
        r = [pltpu.roll(v, SUB - 1, 0) for v in y]
        return [
            jnp.where(last_lane, jnp.where(last_sub, r[(d + 1) % chunks], r[d]), y[d])
            for d in range(chunks)
        ]

    def west(xs):
        y = [pltpu.roll(x, 1, 1) for x in xs]
        r = [pltpu.roll(v, 1, 0) for v in y]
        return [
            jnp.where(first_lane, jnp.where(first_sub, r[d - 1], r[d]), y[d]) for d in range(chunks)
        ]

    def x_copy(i, src, src_row, row, count):
        return pltpu.make_async_copy(
            src.at[:, pl.ds(src_row * 7, count * 7)], x_ref.at[:, pl.ds(row * 7, count * 7)], in_sems.at[i]
        )

    if upper:
        half = (height - CUT) // 2
        arrivals = [
            x_copy(0, x_low, CUT - HALO, CUT - HALO, HALO),
            x_copy(1, x_high, 0, CUT, half),
            x_copy(2, x_high, half, CUT + half, height - CUT - half),
        ]
        in_edges = (CUT, CUT + half, height)
    else:
        in_edges = (CUT // 3, 2 * CUT // 3, CUT)
        arrivals = [
            x_copy(i, x_low, lo, lo, hi - lo) for i, (lo, hi) in enumerate(zip((0, *in_edges), in_edges))
        ]

    def departure(i):
        rows = pl.ds(i * (out_rows // 2) * 6, (out_rows // 2) * 6)
        return pltpu.make_async_copy(out_ref.at[:, rows], out_hbm.at[:, rows], out_sems.at[i])

    def edge(i):
        hbm, ref = ((s1_hbm, s1_ref), (s2_hbm, s2_ref))[i]
        ref = ref.at[:, pl.ds((CUT - 3 - i) * 6, 12)]
        src, dst = (hbm, ref) if upper else (ref, hbm)
        return pltpu.make_async_copy(src, dst, edge_sems.at[i])

    for copy in arrivals:
        copy.start()
    if upper:
        edge(0).start()
        edge(1).start()

    def stage(src, dst, index, fraction):
        fields = 7 if index == 0 else 6
        final = index == 2
        lo, hi = ranges[index]
        in_lo, in_hi = lo - 1, hi + 1
        count = hi - lo + 1

        def get(f, r):
            return [src[d, r * fields + f] for d in range(chunks)]

        def terrain(r):
            return [x_ref[d, r * 7 + 6] for d in range(chunks)]

        def corners(r, carry):
            rn = jnp.minimum(r + 1, in_hi)
            rs = jnp.maximum(r - 1, in_lo)
            c_half, cn_half = coef[0, r] * dy_inv, coef[0, rn] * dy_inv
            e_inv, sine = coef[2, r], coef[3, r]
            h0, h1, ground = get(0, r), get(1, r), terrain(r)
            base = [a + b for a, b in zip(h1, ground)]
            for k in range(2):
                u, v = get(2 + k, r), get(4 + k, r)
                uw, ve = west(u), east(v)
                un, vs = get(2 + k, rn), get(4 + k, rs)
                for d in range(chunks):
                    at = (r * 2 + k) * chunks + d
                    uu_ref[at] = u[d] + uw[d]
                    vv_ref[at] = v[d] + ve[d]
                    kin = 0.25 * (u[d] * u[d] + uw[d] * uw[d] + (v[d] * v[d] + vs[d] * vs[d]))
                    e_ref[at] = kin + (base[d] + (h0[d] if k == 0 else DENSITY_RATIO * h0[d]))
                    curl = (ve[d] - v[d]) - (un[d] * cn_half - u[d] * c_half)
                    z_ref[at] = sine + curl * e_inv
            return carry

        if index == 0:
            first = in_lo
            for i in range(3):
                arrivals[i].wait()
                last = in_edges[i] - 1 if i < 2 else in_edges[i]
                lax.fori_loop(first, last, corners, 0)
                first = last
        else:
            if upper:
                edge(index - 1).wait()
            lax.fori_loop(in_lo, in_hi + 1, corners, 0)

        def tendencies(r, carry):
            c_inv = coef[1, r]
            fn, fs = coef[4, r] * (0.5 * dy_inv), coef[4, r - 1] * (0.5 * dy_inv)
            live = coef[5, r]
            for k in range(2):

                def face(ref, row):
                    return [ref[(row * 2 + k) * chunks + d] for d in range(chunks)]

                def put(f, d, value):
                    start = (d * TILE_ROWS + (r - lo) * 6 + f) * SUB
                    t_ref[pl.ds(pl.multiple_of(start, SUB), SUB), :] = value

                h, hn, hs = get(k, r), get(k, r + 1), get(k, r - 1)
                u, v, vs = get(2 + k, r), get(4 + k, r), get(4 + k, r - 1)
                he = east(h)
                fx = [0.5 * (h[d] + he[d]) * u[d] for d in range(chunks)]
                fxw = west(fx)
                for d in range(chunks):
                    north = (h[d] + hn[d]) * (v[d] * fn) - (h[d] + hs[d]) * (vs[d] * fs)
                    put(k, d, ((fxw[d] - fx[d]) - north) * c_inv)
                z, zs, ec = face(z_ref, r), face(z_ref, r - 1), face(e_ref, r)
                vv, vvs = face(vv_ref, r), face(vv_ref, r - 1)
                ee = east(ec)
                for d in range(chunks):
                    turn = (0.125 * (z[d] + zs[d])) * (vv[d] + vvs[d])
                    put(2 + k, d, turn - (ee[d] - ec[d]) * c_inv)
                en, uu, uun = face(e_ref, r + 1), face(uu_ref, r), face(uu_ref, r + 1)
                zw = west(z)
                for d in range(chunks):
                    turn = (0.125 * (z[d] + zw[d])) * (uu[d] + uun[d])
                    put(4 + k, d, live * (dy_inv * (ec[d] - en[d]) - turn))
            return carry

        lax.fori_loop(lo, hi + 1, tendencies, 0)

        total = -(-6 * count // PAIR)
        units = 2 if total == 4 else 3

        def circle_filter(p, carry):
            wave = lax.broadcasted_iota(jnp.int32, (PAIR, 2 * LANES), 1)
            wave = RADIX * jnp.where(wave >= LANES, wave - LANES, wave)

            def place(unit, a, half):
                d, s = a // SUB, a % SUB
                start = (d * TILE_ROWS + (p * units + unit) * PAIR + half * SUB) * SUB + s
                return pl.ds(start, SUB, stride=SUB)

            def cut_of(unit):
                at = pl.multiple_of((p * units + unit) * PAIR, PAIR)
                return cut_ref[3 * upper + index, pl.ds(at, PAIR), :]

            def analyse(unit, half):
                re, im = real_fft([t_ref[place(unit, a, half), :] for a in range(RADIX)])
                for k in range(HALF + 1):
                    c, s = twc_ref[k : k + 1, :], tws_ref[k : k + 1, :]
                    if k == 0:
                        yr, yi = re[k], jnp.zeros_like(re[k])
                    elif im[k] is None:
                        yr, yi = re[k] * c, -(re[k] * s)
                    else:
                        yr, yi = re[k] * c + im[k] * s, im[k] * c - re[k] * s
                    at = pl.ds((k * 2 + half) * SUB, SUB)
                    y_refs[unit][at, 0:LANES] = yr
                    y_refs[unit][at, LANES : 2 * LANES] = yi

            def product(y, whi, wlo):
                n = y.shape[0]
                hi_part = y.astype(jnp.bfloat16)
                lo_part = (y - hi_part.astype(jnp.float32)).astype(jnp.bfloat16)
                dot = functools.partial(jnp.dot, preferred_element_type=jnp.float32)
                both = dot(jnp.concatenate([hi_part, lo_part], axis=0), whi)
                return both[:n] + both[n:] + dot(hi_part, wlo)

            def mask(unit, start):
                cut = cut_of(unit)
                cut2 = jnp.concatenate([cut, cut], axis=1)
                rows = slice(start * PAIR, (start + BLOCK) * PAIR)
                spec = product(y_refs[unit][rows, :], wfh_ref[...], wfl_ref[...])
                keep = []
                for k in range(start, start + BLOCK):
                    folded = jnp.minimum(wave + k, RADIX * LANES - k - wave)
                    keep.append(folded < cut2)
                spec = jnp.where(jnp.concatenate(keep, axis=0), spec, 0.0)
                y_refs[unit][rows, :] = product(spec, wbh_ref[...], wbl_ref[...])

            def synthesise(unit, half):
                re, im = [], []
                for k in range(HALF + 1):
                    c, s = twc_ref[k : k + 1, :], tws_ref[k : k + 1, :]
                    at = pl.ds((k * 2 + half) * SUB, SUB)
                    yr = y_refs[unit][at, 0:LANES]
                    if k == 0:
                        re.append(yr)
                        im.append(None)
                        continue
                    yi = y_refs[unit][at, LANES : 2 * LANES]
                    re.append(yr * c - yi * s)
                    im.append(None if k == HALF else yr * s + yi * c)
                circles = real_ifft(re, im)
                polar = cut_of(unit)[half * SUB : (half + 1) * SUB] < UNCUT
                for a in range(RADIX):
                    at = place(unit, a, half)
                    t_ref[at, :] = jnp.where(polar, circles[a], t_ref[at, :])

            for unit in range(units):
                for half in range(2):
                    analyse(unit, half)
            for start in range(0, HALF + 1, BLOCK):
                for unit in range(units):
                    mask(unit, start)
            for unit in range(units):
                for half in range(2):
                    synthesise(unit, half)
            return carry

        @pl.when(flags[3 * upper + index] > 0)
        def _():
            lax.fori_loop(0, -(-total // units), circle_filter, 0)

        def update(r, carry):
            inside = coef[6, r]
            for f in range(6):
                for d in range(chunks):
                    start = (d * TILE_ROWS + (r - lo) * 6 + f) * SUB
                    change = t_ref[pl.ds(pl.multiple_of(start, SUB), SUB), :]
                    value = inside * (x_ref[d, r * 7 + f] + (fraction * step_size) * change)
                    if final:
                        out_ref[d, (r - lo) * 6 + f] = value
                    else:
                        dst[d, r * 6 + f] = value
            return carry

        if final:
            for i in range(2):
                lax.fori_loop(lo + i * (count // 2), lo + (i + 1) * (count // 2), update, 0)
                departure(i).start()
        else:
            lax.fori_loop(lo, hi + 1, update, 0)
            if not upper:
                edge(index).start()

    stage(x_ref, s1_ref, 0, 1.0 / 3.0)
    stage(s1_ref, s2_ref, 1, 0.5)
    stage(s2_ref, None, 2, 1.0)
    for i in range(2):
        departure(i).wait()
        if not upper:
            edge(i).wait()


def row_tables(cutoffs, row_start, height, total_rows, polar):
    row_ids = row_start - HALO + jnp.arange(height, dtype=jnp.int32)
    spacing = math.pi / total_rows
    centre_lat = -0.5 * math.pi + (row_ids.astype(jnp.float32) + 0.5) * spacing
    face_lat = -0.5 * math.pi + (row_ids.astype(jnp.float32) + 1.0) * spacing
    inside = jnp.where((row_ids >= 0) & (row_ids < total_rows), 1.0, 0.0).astype(jnp.float32)
    live = jnp.where((row_ids >= 0) & (row_ids < total_rows - 1), 1.0, 0.0).astype(jnp.float32)
    centre_cos = jnp.cos(centre_lat)
    face_cos = jnp.cos(face_lat) * live
    face_inverse = live / (face_cos + (1.0 - live))
    coef = jnp.stack(
        [centre_cos, 1.0 / centre_cos, face_inverse, jnp.sin(face_lat), face_cos, live, inside]
    )
    capped = ((row_ids >= 0) & (row_ids < polar)) | (
        (row_ids >= total_rows - polar) & (row_ids < total_rows)
    )
    position = jnp.where(row_ids < polar, row_ids, row_ids - (total_rows - 2 * polar))
    table_ids = jnp.arange(2 * polar, dtype=jnp.int32)
    cut = jnp.sum(
        jnp.where(position[:, None] == table_ids[None, :], cutoffs[None, :], 0), axis=1, dtype=jnp.int32
    )
    cut = jnp.where(capped, cut, UNCUT)
    stages = []
    for upper in (False, True):
        for lo, hi in stage_rows(height, upper):
            rows = jnp.repeat(cut[lo : hi + 1], 6)
            stages.append(jnp.pad(rows, (0, TILE_ROWS - rows.shape[0]), constant_values=UNCUT))
    cuts = jnp.stack(stages)
    flags = jnp.any(cuts < UNCUT, axis=1).astype(jnp.int32)
    return coef, flags, jnp.broadcast_to(cuts[:, :, None], (6, TILE_ROWS, LANES))


def body(thickness, winds, terrain, cutoffs):
    row_count, col_count = thickness.shape[1], thickness.shape[2]
    bands, sectors = lax.axis_size("lat"), lax.axis_size("lon")
    total_rows, circle = row_count * bands, col_count * sectors
    polar = (total_rows + 2) // 6
    own = row_count // sectors
    height = own + 2 * HALO
    merid_step = circle / (2.0 * total_rows)
    step_size = 0.1 * min(1.0, merid_step)
    lat = lax.axis_index("lat")
    flat = winds.reshape(4, row_count, col_count)

    vmem = pl.BlockSpec(memory_space=pltpu.VMEM)
    smem = pl.BlockSpec(memory_space=pltpu.SMEM)
    hbm = pl.BlockSpec(memory_space=pltpu.HBM)
    rim = jax.ShapeDtypeStruct((HALO * 7 * SUB, LANES), jnp.float32)
    tail, head = pl.pallas_call(
        edge_kernel,
        out_shape=(rim, rim),
        in_specs=[hbm] * 3,
        out_specs=(vmem, vmem),
        scratch_shapes=[
            pltpu.VMEM((2, 7, SUB, col_count), jnp.float32),
            pltpu.SemaphoreType.DMA((2, 7)),
        ],
        name="edge",
    )(thickness, flat, terrain)
    south = lax.ppermute(tail, "lat", [(i, i + 1) for i in range(bands - 1)])
    north = lax.ppermute(head, "lat", [(i + 1, i) for i in range(bands - 1)])

    def piece(rows, fields):
        return jax.ShapeDtypeStruct((sectors, rows * fields * SUB, LANES), jnp.float32)

    packed_low, packed_high = pl.pallas_call(
        functools.partial(pack_kernel, bands),
        out_shape=(piece(CUT, 7), piece(height - CUT, 7)),
        in_specs=[smem] + [hbm] * 3,
        out_specs=(hbm, hbm),
        scratch_shapes=[
            pltpu.VMEM(thickness.shape, jnp.float32),
            pltpu.VMEM(flat.shape, jnp.float32),
            pltpu.VMEM(terrain.shape, jnp.float32),
            pltpu.VMEM(piece(height, 7).shape, jnp.float32),
            pltpu.SemaphoreType.DMA((3, sectors)),
            pltpu.SemaphoreType.DMA((2, sectors)),
        ],
        compiler_params=pltpu.CompilerParams(vmem_limit_bytes=56 << 20),
        cost_estimate=pl.CostEstimate(flops=0, bytes_accessed=12 << 20, transcendentals=0),
        name="pack",
    )(lat.reshape(1).astype(jnp.int32), thickness, flat, terrain)

    def rimmed(packed, rows, group, start):
        return pl.pallas_call(
            functools.partial(rim_kernel, group, start),
            out_shape=jax.ShapeDtypeStruct(packed.shape, jnp.float32),
            in_specs=[pl.BlockSpec(memory_space=pl.ANY), hbm],
            out_specs=hbm,
            scratch_shapes=[pltpu.SemaphoreType.DMA],
            input_output_aliases={1: 0},
            name="rim",
        )(rows, packed)

    packed_low = rimmed(packed_low, south, 0, 0)
    packed_high = rimmed(packed_high, north, sectors - 1, (HALO + own - CUT) * 7 * SUB)
    circles_low = lax.all_to_all(packed_low, "lon", 0, 0)
    circles_high = lax.all_to_all(packed_high, "lon", 0, 0)

    row_start = lat * row_count + lax.axis_index("lon") * own
    coef, flags, cuts = row_tables(cutoffs, row_start, height, total_rows, polar)
    tables = [jnp.asarray(t) for t in filter_tables()]
    edges = jax.ShapeDtypeStruct((sectors, 12, SUB, LANES), jnp.float32)

    def step(upper, states, saved):
        lo, hi = stage_rows(height, upper)[2]
        out = jax.ShapeDtypeStruct((sectors, 6 * (hi - lo + 1), SUB, LANES), jnp.float32)
        states = [x.reshape(sectors, -1, SUB, LANES) for x in states]
        return pl.pallas_call(
            functools.partial(step_kernel, upper, height, merid_step, step_size),
            out_shape=out if upper else (out, edges, edges),
            in_specs=[smem, smem] + [hbm] * len(states + saved) + [vmem] * 7,
            out_specs=hbm if upper else (hbm, hbm, hbm),
            scratch_shapes=[
                pltpu.VMEM((sectors, 7 * height, SUB, LANES), jnp.float32),
                pltpu.VMEM((sectors, 6 * height, SUB, LANES), jnp.float32),
                pltpu.VMEM((sectors, 6 * height, SUB, LANES), jnp.float32),
                pltpu.VMEM(out.shape, jnp.float32),
                pltpu.VMEM((sectors * TILE_ROWS * SUB, LANES), jnp.float32),
                pltpu.SemaphoreType.DMA((3,)),
                pltpu.SemaphoreType.DMA((2,)),
                pltpu.SemaphoreType.DMA((2,)),
            ]
            + [pltpu.VMEM((height * 2 * sectors, SUB, LANES), jnp.float32)] * 4
            + [pltpu.VMEM(((HALF + 1) * PAIR, 2 * LANES), jnp.float32)] * UNITS,
            compiler_params=pltpu.CompilerParams(vmem_limit_bytes=50 << 20),
            cost_estimate=pl.CostEstimate(flops=0, bytes_accessed=64 << 20, transcendentals=0),
            name="step_high" if upper else "step_low",
        )(coef, flags, *states, *saved, cuts, *tables)

    new_low, *saved = step(False, [circles_low], [])
    returned_low = lax.all_to_all(new_low.reshape(sectors, -1, LANES), "lon", 0, 0)
    new_high = step(True, [circles_low, circles_high], saved)
    returned_high = lax.all_to_all(new_high.reshape(sectors, -1, LANES), "lon", 0, 0)

    def unpack(first, pieces, outputs):
        rows = pieces.shape[1] // (6 * SUB)
        return pl.pallas_call(
            functools.partial(unpack_kernel, first),
            out_shape=(
                jax.ShapeDtypeStruct(thickness.shape, jnp.float32),
                jax.ShapeDtypeStruct(flat.shape, jnp.float32),
            ),
            in_specs=[vmem] + [hbm] * len(outputs),
            out_specs=(hbm, hbm),
            scratch_shapes=[
                pltpu.VMEM((6, sectors, rows, col_count), jnp.float32),
                pltpu.SemaphoreType.DMA((6, sectors)),
            ],
            input_output_aliases={1: 0, 2: 1} if outputs else {},
            compiler_params=pltpu.CompilerParams(vmem_limit_bytes=40 << 20),
            cost_estimate=pl.CostEstimate(flops=0, bytes_accessed=4 << 20, transcendentals=0),
            name="unpack",
        )(pieces, *outputs)

    outputs = unpack(0, returned_low, ())
    new_thickness, new_winds = unpack(own // 2, returned_high, outputs)
    return new_thickness, new_winds.reshape(winds.shape)


def solution(mesh):
    in_specs = (P(None, "lat", "lon"), P(None, None, "lat", "lon"), P("lat", "lon"), P())
    out_specs = (P(None, "lat", "lon"), P(None, None, "lat", "lon"))
    return jax.shard_map(body, mesh=mesh, in_specs=in_specs, out_specs=out_specs, check_vma=False)
```

```python
import functools
import math

import jax
import jax.numpy as jnp
import ml_dtypes
import numpy as np
from jax import lax
from jax.experimental import pallas as pl
from jax.experimental.pallas import tpu as pltpu
from jax.sharding import PartitionSpec as P

DENSITY_RATIO = 0.9
HALO = 3
SUB = 8
LANES = 128
RADIX = 64
HALF = RADIX // 2
UNCUT = 1 << 20
TILE_ROWS = 96
PAIR = 16
UNITS = 3
BLOCK = 11
INNER = 14


def twisted(real, imag, k, n):
    angle = 2.0 * math.pi * k / n
    c, s = math.cos(angle), math.sin(angle)
    if k == 0:
        return real, imag
    if 8 * k == n:
        return (real + imag) * c, (imag - real) * c
    if 8 * k == 3 * n:
        return (imag - real) * s, -(real + imag) * s
    return real * c + imag * s, imag * c - real * s


def real_fft(x):
    n = len(x)
    if n == 1:
        return [x[0]], [None]
    er, ei = real_fft(x[0::2])
    odr, odi = real_fft(x[1::2])
    half = n // 2
    re, im = [None] * (half + 1), [None] * (half + 1)
    re[0], re[half] = er[0] + odr[0], er[0] - odr[0]
    for k in range(1, half // 2 + 1):
        if 2 * k == half:
            re[k], im[k] = er[k], -odr[k]
            continue
        tr, ti = twisted(odr[k], odi[k], k, n)
        re[k], im[k] = er[k] + tr, ei[k] + ti
        re[half - k], im[half - k] = er[k] - tr, ti - ei[k]
    return re, im


def real_ifft(re, im):
    n = 2 * (len(re) - 1)
    if n == 0:
        return [re[0]]
    half = n // 2
    if n == 2:
        return [re[0] + re[1], re[0] - re[1]]
    quarter = half // 2
    er, ei = [None] * (quarter + 1), [None] * (quarter + 1)
    odr, odi = [None] * (quarter + 1), [None] * (quarter + 1)
    er[0], odr[0] = re[0] + re[half], re[0] - re[half]
    for k in range(1, quarter + 1):
        if k == quarter:
            er[k], odr[k] = 2.0 * re[k], -2.0 * im[k]
            continue
        sr, si = re[k] + re[half - k], im[k] - im[half - k]
        dr, di = re[k] - re[half - k], im[k] + im[half - k]
        er[k], ei[k] = sr, si
        odi[k], odr[k] = twisted(di, dr, k, n)
    even = real_ifft(er, ei)
    odd = real_ifft(odr, odi)
    out = [None] * n
    out[0::2], out[1::2] = even, odd
    return out


def filter_tables():
    b = np.arange(LANES)
    angle = 2.0 * np.pi * (np.outer(b, b) % LANES) / LANES
    c, s = np.cos(angle), np.sin(angle)
    forward = np.block([[c, -s], [s, c]])
    backward = forward.T / (RADIX * LANES)

    def split(w):
        hi = w.astype(np.float32).astype(ml_dtypes.bfloat16)
        lo = (w - hi.astype(np.float64)).astype(np.float32).astype(ml_dtypes.bfloat16)
        return hi, lo

    k1 = np.arange(40)[:, None]
    twist = 2.0 * np.pi * k1 * b[None, :] / (RADIX * LANES)
    return (
        *split(forward),
        *split(backward),
        np.cos(twist).astype(np.float32),
        np.sin(twist).astype(np.float32),
    )


def edge_kernel(th_ref, wi_ref, te_ref, tail_ref, head_ref, tile_ref, sems):
    rows = te_ref.shape[0]

    def copies(f):
        src = th_ref.at[f] if f < 2 else wi_ref.at[f - 2] if f < 6 else te_ref
        return [
            pltpu.make_async_copy(src.at[pl.ds(start, SUB)], tile_ref.at[i, f], sems.at[i, f])
            for i, start in enumerate((rows - SUB, 0))
        ]

    for f in range(7):
        for copy in copies(f):
            copy.start()
    for f in range(7):
        for i, copy in enumerate(copies(f)):
            copy.wait()
            out_ref, start = ((tail_ref, SUB - HALO), (head_ref, 0))[i]
            for s in range(SUB):
                out_ref[pl.ds(f * SUB + s, HALO, stride=7 * SUB), :] = tile_ref[
                    i, f, start : start + HALO, s * LANES : (s + 1) * LANES
                ]


def pack_kernel(bands, lat_ref, th_hbm, wi_hbm, te_hbm, a_hbm, b_hbm, th_ref, wi_ref, te_ref, piece_ref, in_sems, sems):
    groups = piece_ref.shape[0]
    height = piece_ref.shape[1] // (7 * SUB)
    own = height - 2 * HALO
    def arrivals(g):
        rows = pl.ds(g * own, own)
        return (
            pltpu.make_async_copy(th_hbm.at[:, rows], th_ref.at[:, rows], in_sems.at[0, g]),
            pltpu.make_async_copy(wi_hbm.at[:, rows], wi_ref.at[:, rows], in_sems.at[1, g]),
            pltpu.make_async_copy(te_hbm.at[rows], te_ref.at[rows], in_sems.at[2, g]),
        )

    def departures(g):
        def copy(i, dst, src_row, dst_row, count):
            src = piece_ref.at[g, pl.ds(src_row * 7 * SUB, count * 7 * SUB)]
            dst = dst.at[g, pl.ds(dst_row * 7 * SUB, count * 7 * SUB)]
            return pltpu.make_async_copy(src, dst, sems.at[i, g])

        top = HALO + INNER
        last = height if g < groups - 1 else HALO + own
        copies = [copy(0, a_hbm, HALO, 0, INNER), copy(1, b_hbm, top, HALO, last - top)]
        return copies + ([copy(2, b_hbm, 0, 0, HALO)] if g > 0 else [])

    for g in range(groups):
        for copy in arrivals(g):
            copy.start()
    for copy in arrivals(0):
        copy.wait()
    for g in range(groups):
        if g < groups - 1:
            for copy in arrivals(g + 1):
                copy.wait()
        for f in range(7):
            src = th_ref.at[f] if f < 2 else wi_ref.at[f - 2] if f < 6 else te_ref

            def put(dst, start, count):
                for s in range(SUB):
                    piece_ref[g, pl.ds((dst * 7 + f) * SUB + s, count, stride=7 * SUB), :] = src[
                        pl.ds(start, count), s * LANES : (s + 1) * LANES
                    ]

            for m in range(own // SUB):
                put(HALO + m * SUB, g * own + m * SUB, SUB)
            if g > 0:
                put(0, g * own - HALO, HALO)
            if g < groups - 1:
                put(HALO + own, (g + 1) * own, HALO)
        if g == groups - 1:

            @pl.when(lat_ref[0] == bands - 1)
            def _():
                for f in (4, 5):
                    at = pl.ds(((HALO + own - 1) * 7 + f) * SUB, SUB)
                    piece_ref[g, at, :] = jnp.zeros((SUB, LANES), jnp.float32)

        for copy in departures(g):
            copy.start()
    for g in range(groups):
        for copy in departures(g):
            copy.wait()


def rim_kernel(south_ref, north_ref, packed_ref, out_ref, sems):
    groups, length = out_ref.shape[0], out_ref.shape[1]
    rim = HALO * 7 * SUB
    low = pltpu.make_async_copy(south_ref, out_ref.at[0, pl.ds(0, rim)], sems.at[0])
    high = pltpu.make_async_copy(north_ref, out_ref.at[groups - 1, pl.ds(length - rim, rim)], sems.at[1])
    low.start()
    high.start()
    low.wait()
    high.wait()


def unpack_kernel(low_ref, high_ref, th_hbm, wi_hbm, tile_ref, sems):
    groups = low_ref.shape[0]
    low_rows, high_rows = (r.shape[1] // (6 * SUB) for r in (low_ref, high_ref))
    own = low_rows + high_rows
    spans = (
        (low_ref, 0, HALO, low_rows),
        (high_ref, 0, 0, HALO),
        (high_ref, HALO, HALO + low_rows, high_rows - HALO),
    )

    def departure(f):
        dst = th_hbm.at[f] if f < 2 else wi_hbm.at[f - 2]
        return pltpu.make_async_copy(tile_ref.at[f], dst, sems.at[f])

    for f in range(6):
        for g in range(groups):
            for src, src_row, row, count in spans:
                for s in range(SUB):
                    tile_ref[f, pl.ds(g * own + row, count), s * LANES : (s + 1) * LANES] = src[
                        g, pl.ds((src_row * 6 + f) * SUB + s, count, stride=6 * SUB), :
                    ]
        departure(f).start()
    for f in range(6):
        departure(f).wait()


def stage_rows(height, outer):
    top = HALO + INNER
    if outer:
        return [((1 + k, HALO + k), (top - 1 - k, height - 2 - k)) for k in range(3)]
    return [((HALO + 1 + k, top - 2 - k),) for k in range(3)]


def step_kernel(outer, height, merid_step, step_size, coef, flags, *refs):
    if outer:
        x_low, x_high, s1_hbm, s2_hbm, *refs = refs
    else:
        x_low, *refs = refs
    cut_ref, wfh_ref, wfl_ref, wbh_ref, wbl_ref, twc_ref, tws_ref, *refs = refs
    out_hbm, *refs = refs
    if not outer:
        s1_hbm, s2_hbm, *refs = refs
    x_ref, s1_ref, s2_ref, out_ref, t_ref, in_sems, out_sems, edge_sems, *refs = refs
    e_ref, z_ref, uu_ref, vv_ref, *y_refs = refs
    chunks = x_ref.shape[0]
    ranges = stage_rows(height, outer)
    top = HALO + INNER
    lane = lax.broadcasted_iota(jnp.int32, (SUB, LANES), 1)
    sub = lax.broadcasted_iota(jnp.int32, (SUB, LANES), 0)
    last_lane, first_lane = lane == LANES - 1, lane == 0
    last_sub, first_sub = sub == SUB - 1, sub == 0
    dy_inv = 1.0 / merid_step

    def east(xs):
        y = [pltpu.roll(x, LANES - 1, 1) for x in xs]
        r = [pltpu.roll(v, SUB - 1, 0) for v in y]
        return [
            jnp.where(last_lane, jnp.where(last_sub, r[(d + 1) % chunks], r[d]), y[d])
            for d in range(chunks)
        ]

    def west(xs):
        y = [pltpu.roll(x, 1, 1) for x in xs]
        r = [pltpu.roll(v, 1, 0) for v in y]
        return [
            jnp.where(first_lane, jnp.where(first_sub, r[d - 1], r[d]), y[d]) for d in range(chunks)
        ]

    def x_copy(i, src, src_row, row, count):
        return pltpu.make_async_copy(
            src.at[:, pl.ds(src_row * 7, count * 7)], x_ref.at[:, pl.ds(row * 7, count * 7)], in_sems.at[i]
        )

    if outer:
        arrivals = [
            [x_copy(0, x_high, 0, 0, HALO), x_copy(1, x_low, 0, HALO, HALO)],
            [x_copy(2, x_low, INNER - HALO, top - HALO, HALO), x_copy(3, x_high, HALO, top, height - top)],
        ]
        out_edges = (0, HALO, height - 2 * HALO - (INNER - 6))
    else:
        bounds = (0, INNER // 3, 2 * INNER // 3, INNER)
        arrivals = [
            [x_copy(i, x_low, lo, HALO + lo, hi - lo)] for i, (lo, hi) in enumerate(zip(bounds, bounds[1:]))
        ]
        out_edges = (0, (INNER - 6) // 2, INNER - 6)

    def departure(i):
        rows = pl.ds(out_edges[i] * 6, (out_edges[i + 1] - out_edges[i]) * 6)
        return pltpu.make_async_copy(out_ref.at[:, rows], out_hbm.at[:, rows], out_sems.at[i])

    def edges(index):
        hbm, ref = ((s1_hbm, s1_ref), (s2_hbm, s2_ref))[index]
        copies = []
        for i, row in enumerate((HALO + 1 + index, top - 3 - index)):
            src, dst = hbm.at[:, pl.ds(i * 12, 12)], ref.at[:, pl.ds(row * 6, 12)]
            src, dst = (src, dst) if outer else (dst, src)
            copies.append(pltpu.make_async_copy(src, dst, edge_sems.at[index, i]))
        return copies

    for copy in sum(arrivals, []):
        copy.start()
    if outer:
        for copy in edges(0) + edges(1):
            copy.start()

    def stage(src, dst, index, fraction):
        fields = 7 if index == 0 else 6
        final = index == 2
        count = sum(hi - lo + 1 for lo, hi in ranges[index])

        def get(f, r):
            return [src[d, r * fields + f] for d in range(chunks)]

        def terrain(r):
            return [x_ref[d, r * 7 + 6] for d in range(chunks)]

        def corners(in_lo, in_hi, r, carry):
            rn = jnp.minimum(r + 1, in_hi)
            rs = jnp.maximum(r - 1, in_lo)
            c_half, cn_half = coef[0, r] * dy_inv, coef[0, rn] * dy_inv
            e_inv, sine = coef[2, r], coef[3, r]
            h0, h1, ground = get(0, r), get(1, r), terrain(r)
            base = [a + b for a, b in zip(h1, ground)]
            for k in range(2):
                u, v = get(2 + k, r), get(4 + k, r)
                uw, ve = west(u), east(v)
                un, vs = get(2 + k, rn), get(4 + k, rs)
                for d in range(chunks):
                    at = (r * 2 + k) * chunks + d
                    uu_ref[at] = u[d] + uw[d]
                    vv_ref[at] = v[d] + ve[d]
                    kin = 0.25 * (u[d] * u[d] + uw[d] * uw[d] + (v[d] * v[d] + vs[d] * vs[d]))
                    e_ref[at] = kin + (base[d] + (h0[d] if k == 0 else DENSITY_RATIO * h0[d]))
                    curl = (ve[d] - v[d]) - (un[d] * cn_half - u[d] * c_half)
                    z_ref[at] = sine + curl * e_inv
            return carry

        def tendencies(shift, r, carry):
            c_inv = coef[1, r]
            fn, fs = coef[4, r] * (0.5 * dy_inv), coef[4, r - 1] * (0.5 * dy_inv)
            live = coef[5, r]
            for k in range(2):

                def face(ref, row):
                    return [ref[(row * 2 + k) * chunks + d] for d in range(chunks)]

                def put(f, d, value):
                    start = (d * TILE_ROWS + (r - shift) * 6 + f) * SUB
                    t_ref[pl.ds(pl.multiple_of(start, SUB), SUB), :] = value

                h, hn, hs = get(k, r), get(k, r + 1), get(k, r - 1)
                u, v, vs = get(2 + k, r), get(4 + k, r), get(4 + k, r - 1)
                he = east(h)
                fx = [0.5 * (h[d] + he[d]) * u[d] for d in range(chunks)]
                fxw = west(fx)
                for d in range(chunks):
                    north = (h[d] + hn[d]) * (v[d] * fn) - (h[d] + hs[d]) * (vs[d] * fs)
                    put(k, d, ((fxw[d] - fx[d]) - north) * c_inv)
                z, zs, ec = face(z_ref, r), face(z_ref, r - 1), face(e_ref, r)
                vv, vvs = face(vv_ref, r), face(vv_ref, r - 1)
                ee = east(ec)
                for d in range(chunks):
                    turn = (0.125 * (z[d] + zs[d])) * (vv[d] + vvs[d])
                    put(2 + k, d, turn - (ee[d] - ec[d]) * c_inv)
                en, uu, uun = face(e_ref, r + 1), face(uu_ref, r), face(uu_ref, r + 1)
                zw = west(z)
                for d in range(chunks):
                    turn = (0.125 * (z[d] + zw[d])) * (uu[d] + uun[d])
                    put(4 + k, d, live * (dy_inv * (ec[d] - en[d]) - turn))
            return carry

        if index > 0 and outer:
            for copy in edges(index - 1):
                copy.wait()
        base = 0
        for i, (lo, hi) in enumerate(ranges[index]):
            calc = functools.partial(corners, lo - 1, hi + 1)
            if index > 0:
                lax.fori_loop(lo - 1, hi + 2, calc, 0)
            elif outer:
                for copy in arrivals[i]:
                    copy.wait()
                lax.fori_loop(lo - 1, hi + 2, calc, 0)
            else:
                first = lo - 1
                for j, (copy,) in enumerate(arrivals):
                    copy.wait()
                    last = HALO + bounds[j + 1] - (1 if j < 2 else 0)
                    lax.fori_loop(first, last, calc, 0)
                    first = last
            lax.fori_loop(lo, hi + 1, functools.partial(tendencies, lo - base), 0)
            base += hi - lo + 1

        total = -(-6 * count // PAIR)
        units = 2 if total == 4 else 3

        def circle_filter(p, carry):
            wave = lax.broadcasted_iota(jnp.int32, (PAIR, 2 * LANES), 1)
            wave = RADIX * jnp.where(wave >= LANES, wave - LANES, wave)

            def place(unit, a, half):
                d, s = a // SUB, a % SUB
                start = (d * TILE_ROWS + (p * units + unit) * PAIR + half * SUB) * SUB + s
                return pl.ds(start, SUB, stride=SUB)

            def cut_of(unit):
                at = pl.multiple_of((p * units + unit) * PAIR, PAIR)
                return cut_ref[3 * outer + index, pl.ds(at, PAIR), :]

            def analyse(unit, half):
                re, im = real_fft([t_ref[place(unit, a, half), :] for a in range(RADIX)])
                for k in range(HALF + 1):
                    c, s = twc_ref[k : k + 1, :], tws_ref[k : k + 1, :]
                    if k == 0:
                        yr, yi = re[k], jnp.zeros_like(re[k])
                    elif im[k] is None:
                        yr, yi = re[k] * c, -(re[k] * s)
                    else:
                        yr, yi = re[k] * c + im[k] * s, im[k] * c - re[k] * s
                    at = pl.ds((k * 2 + half) * SUB, SUB)
                    y_refs[unit][at, 0:LANES] = yr
                    y_refs[unit][at, LANES : 2 * LANES] = yi

            def product(y, whi, wlo):
                n = y.shape[0]
                hi_part = y.astype(jnp.bfloat16)
                lo_part = (y - hi_part.astype(jnp.float32)).astype(jnp.bfloat16)
                dot = functools.partial(jnp.dot, preferred_element_type=jnp.float32)
                both = dot(jnp.concatenate([hi_part, lo_part], axis=0), whi)
                return both[:n] + both[n:] + dot(hi_part, wlo)

            def mask(unit, start):
                cut = cut_of(unit)
                cut2 = jnp.concatenate([cut, cut], axis=1)
                rows = slice(start * PAIR, (start + BLOCK) * PAIR)
                spec = product(y_refs[unit][rows, :], wfh_ref[...], wfl_ref[...])
                keep = []
                for k in range(start, start + BLOCK):
                    folded = jnp.minimum(wave + k, RADIX * LANES - k - wave)
                    keep.append(folded < cut2)
                spec = jnp.where(jnp.concatenate(keep, axis=0), spec, 0.0)
                y_refs[unit][rows, :] = product(spec, wbh_ref[...], wbl_ref[...])

            def synthesise(unit, half):
                re, im = [], []
                for k in range(HALF + 1):
                    c, s = twc_ref[k : k + 1, :], tws_ref[k : k + 1, :]
                    at = pl.ds((k * 2 + half) * SUB, SUB)
                    yr = y_refs[unit][at, 0:LANES]
                    if k == 0:
                        re.append(yr)
                        im.append(None)
                        continue
                    yi = y_refs[unit][at, LANES : 2 * LANES]
                    re.append(yr * c - yi * s)
                    im.append(None if k == HALF else yr * s + yi * c)
                circles = real_ifft(re, im)
                polar = cut_of(unit)[half * SUB : (half + 1) * SUB] < UNCUT
                for a in range(RADIX):
                    at = place(unit, a, half)
                    t_ref[at, :] = jnp.where(polar, circles[a], t_ref[at, :])

            for unit in range(units):
                for half in range(2):
                    analyse(unit, half)
            for start in range(0, HALF + 1, BLOCK):
                for unit in range(units):
                    mask(unit, start)
            for unit in range(units):
                for half in range(2):
                    synthesise(unit, half)
            return carry

        @pl.when(flags[3 * outer + index] > 0)
        def _():
            lax.fori_loop(0, -(-total // units), circle_filter, 0)

        def update(shift, r, carry):
            inside = coef[6, r]
            for f in range(6):
                for d in range(chunks):
                    start = (d * TILE_ROWS + (r - shift) * 6 + f) * SUB
                    change = t_ref[pl.ds(pl.multiple_of(start, SUB), SUB), :]
                    value = inside * (x_ref[d, r * 7 + f] + (fraction * step_size) * change)
                    if final:
                        out_ref[d, (r - shift) * 6 + f] = value
                    else:
                        dst[d, r * 6 + f] = value
            return carry

        spans = ranges[index]
        if final and not outer:
            (lo, hi), middle = spans[0], spans[0][0] + out_edges[1]
            spans = ((lo, middle - 1), (middle, hi))
        base = 0
        for i, (lo, hi) in enumerate(spans):
            lax.fori_loop(lo, hi + 1, functools.partial(update, lo - base), 0)
            base += hi - lo + 1
            if final:
                departure(i).start()
        if not final and not outer:
            for copy in edges(index):
                copy.start()

    stage(x_ref, s1_ref, 0, 1.0 / 3.0)
    stage(s1_ref, s2_ref, 1, 0.5)
    stage(s2_ref, None, 2, 1.0)
    for i in range(2):
        departure(i).wait()
        if not outer:
            for copy in edges(i):
                copy.wait()


def row_tables(cutoffs, row_start, height, total_rows, polar):
    row_ids = row_start - HALO + jnp.arange(height, dtype=jnp.int32)
    spacing = math.pi / total_rows
    centre_lat = -0.5 * math.pi + (row_ids.astype(jnp.float32) + 0.5) * spacing
    face_lat = -0.5 * math.pi + (row_ids.astype(jnp.float32) + 1.0) * spacing
    inside = jnp.where((row_ids >= 0) & (row_ids < total_rows), 1.0, 0.0).astype(jnp.float32)
    live = jnp.where((row_ids >= 0) & (row_ids < total_rows - 1), 1.0, 0.0).astype(jnp.float32)
    centre_cos = jnp.cos(centre_lat)
    face_cos = jnp.cos(face_lat) * live
    face_inverse = live / (face_cos + (1.0 - live))
    coef = jnp.stack(
        [centre_cos, 1.0 / centre_cos, face_inverse, jnp.sin(face_lat), face_cos, live, inside]
    )
    capped = ((row_ids >= 0) & (row_ids < polar)) | (
        (row_ids >= total_rows - polar) & (row_ids < total_rows)
    )
    position = jnp.where(row_ids < polar, row_ids, row_ids - (total_rows - 2 * polar))
    table_ids = jnp.arange(2 * polar, dtype=jnp.int32)
    cut = jnp.sum(
        jnp.where(position[:, None] == table_ids[None, :], cutoffs[None, :], 0), axis=1, dtype=jnp.int32
    )
    cut = jnp.where(capped, cut, UNCUT)
    stages = []
    for outer in (False, True):
        for spans in stage_rows(height, outer):
            rows = jnp.repeat(jnp.concatenate([cut[lo : hi + 1] for lo, hi in spans]), 6)
            stages.append(jnp.pad(rows, (0, TILE_ROWS - rows.shape[0]), constant_values=UNCUT))
    cuts = jnp.stack(stages)
    flags = jnp.any(cuts < UNCUT, axis=1).astype(jnp.int32)
    return coef, flags, jnp.broadcast_to(cuts[:, :, None], (6, TILE_ROWS, LANES))


def body(thickness, winds, terrain, cutoffs):
    row_count, col_count = thickness.shape[1], thickness.shape[2]
    bands, sectors = lax.axis_size("lat"), lax.axis_size("lon")
    total_rows, circle = row_count * bands, col_count * sectors
    polar = (total_rows + 2) // 6
    own = row_count // sectors
    height = own + 2 * HALO
    merid_step = circle / (2.0 * total_rows)
    step_size = 0.1 * min(1.0, merid_step)
    lat = lax.axis_index("lat")
    flat = winds.reshape(4, row_count, col_count)

    vmem = pl.BlockSpec(memory_space=pltpu.VMEM)
    smem = pl.BlockSpec(memory_space=pltpu.SMEM)
    hbm = pl.BlockSpec(memory_space=pltpu.HBM)
    rim = jax.ShapeDtypeStruct((HALO * 7 * SUB, LANES), jnp.float32)
    tail, head = pl.pallas_call(
        edge_kernel,
        out_shape=(rim, rim),
        in_specs=[hbm] * 3,
        out_specs=(vmem, vmem),
        scratch_shapes=[
            pltpu.VMEM((2, 7, SUB, col_count), jnp.float32),
            pltpu.SemaphoreType.DMA((2, 7)),
        ],
        name="edge",
    )(thickness, flat, terrain)
    south = lax.ppermute(tail, "lat", [(i, i + 1) for i in range(bands - 1)])
    north = lax.ppermute(head, "lat", [(i + 1, i) for i in range(bands - 1)])

    def piece(rows, fields):
        return jax.ShapeDtypeStruct((sectors, rows * fields * SUB, LANES), jnp.float32)

    packed_low, packed_high = pl.pallas_call(
        functools.partial(pack_kernel, bands),
        out_shape=(piece(INNER, 7), piece(height - INNER, 7)),
        in_specs=[smem] + [hbm] * 3,
        out_specs=(hbm, hbm),
        scratch_shapes=[
            pltpu.VMEM(thickness.shape, jnp.float32),
            pltpu.VMEM(flat.shape, jnp.float32),
            pltpu.VMEM(terrain.shape, jnp.float32),
            pltpu.VMEM(piece(height, 7).shape, jnp.float32),
            pltpu.SemaphoreType.DMA((3, sectors)),
            pltpu.SemaphoreType.DMA((3, sectors)),
        ],
        compiler_params=pltpu.CompilerParams(vmem_limit_bytes=56 << 20),
        cost_estimate=pl.CostEstimate(flops=0, bytes_accessed=12 << 20, transcendentals=0),
        name="pack",
    )(lat.reshape(1).astype(jnp.int32), thickness, flat, terrain)

    packed_high = pl.pallas_call(
        rim_kernel,
        out_shape=jax.ShapeDtypeStruct(packed_high.shape, jnp.float32),
        in_specs=[vmem, vmem, hbm],
        out_specs=hbm,
        scratch_shapes=[pltpu.SemaphoreType.DMA((2,))],
        input_output_aliases={2: 0},
        name="rim",
    )(south, north, packed_high)
    circles_low = lax.all_to_all(packed_low, "lon", 0, 0)
    circles_high = lax.all_to_all(packed_high, "lon", 0, 0)

    row_start = lat * row_count + lax.axis_index("lon") * own
    coef, flags, cuts = row_tables(cutoffs, row_start, height, total_rows, polar)
    tables = [jnp.asarray(t) for t in filter_tables()]
    edges = jax.ShapeDtypeStruct((sectors, 24, SUB, LANES), jnp.float32)

    def step(outer, states, saved):
        rows = sum(hi - lo + 1 for lo, hi in stage_rows(height, outer)[2])
        out = jax.ShapeDtypeStruct((sectors, 6 * rows, SUB, LANES), jnp.float32)
        states = [x.reshape(sectors, -1, SUB, LANES) for x in states]
        return pl.pallas_call(
            functools.partial(step_kernel, outer, height, merid_step, step_size),
            out_shape=out if outer else (out, edges, edges),
            in_specs=[smem, smem] + [hbm] * len(states + saved) + [vmem] * 7,
            out_specs=hbm if outer else (hbm, hbm, hbm),
            scratch_shapes=[
                pltpu.VMEM((sectors, 7 * height, SUB, LANES), jnp.float32),
                pltpu.VMEM((sectors, 6 * height, SUB, LANES), jnp.float32),
                pltpu.VMEM((sectors, 6 * height, SUB, LANES), jnp.float32),
                pltpu.VMEM(out.shape, jnp.float32),
                pltpu.VMEM((sectors * TILE_ROWS * SUB, LANES), jnp.float32),
                pltpu.SemaphoreType.DMA((4,)),
                pltpu.SemaphoreType.DMA((2,)),
                pltpu.SemaphoreType.DMA((2, 2)),
            ]
            + [pltpu.VMEM((height * 2 * sectors, SUB, LANES), jnp.float32)] * 4
            + [pltpu.VMEM(((HALF + 1) * PAIR, 2 * LANES), jnp.float32)] * UNITS,
            compiler_params=pltpu.CompilerParams(vmem_limit_bytes=53 << 20),
            cost_estimate=pl.CostEstimate(flops=0, bytes_accessed=64 << 20, transcendentals=0),
            name="step_outer" if outer else "step_inner",
        )(coef, flags, *states, *saved, cuts, *tables)

    new_low, *saved = step(False, [circles_low], [])
    returned_low = lax.all_to_all(new_low.reshape(sectors, -1, LANES), "lon", 0, 0)
    new_high = step(True, [circles_low, circles_high], saved)
    returned_low, new_high = lax.optimization_barrier((returned_low, new_high))
    returned_high = lax.all_to_all(new_high.reshape(sectors, -1, LANES), "lon", 0, 0)

    new_thickness, new_winds = pl.pallas_call(
        unpack_kernel,
        out_shape=(
            jax.ShapeDtypeStruct(thickness.shape, jnp.float32),
            jax.ShapeDtypeStruct(flat.shape, jnp.float32),
        ),
        in_specs=[vmem, vmem],
        out_specs=(hbm, hbm),
        scratch_shapes=[
            pltpu.VMEM((6, row_count, col_count), jnp.float32),
            pltpu.SemaphoreType.DMA((6,)),
        ],
        compiler_params=pltpu.CompilerParams(vmem_limit_bytes=40 << 20),
        name="unpack",
    )(returned_low, returned_high)
    return new_thickness, new_winds.reshape(winds.shape)


def solution(mesh):
    in_specs = (P(None, "lat", "lon"), P(None, None, "lat", "lon"), P("lat", "lon"), P())
    out_specs = (P(None, "lat", "lon"), P(None, None, "lat", "lon"))
    return jax.shard_map(body, mesh=mesh, in_specs=in_specs, out_specs=out_specs, check_vma=False)
```

```python
import functools
import math

import jax
import jax.numpy as jnp
import ml_dtypes
import numpy as np
from jax import lax
from jax.experimental import pallas as pl
from jax.experimental.pallas import tpu as pltpu
from jax.sharding import PartitionSpec as P

DENSITY_RATIO = 0.9
HALO = 3
SUB = 8
LANES = 128
RADIX = 64
HALF = RADIX // 2
UNCUT = 1 << 20
TILE_ROWS = 96
PAIR = 16
UNITS = 3
BLOCK = 11
INNER = 14


def twisted(real, imag, k, n):
    angle = 2.0 * math.pi * k / n
    c, s = math.cos(angle), math.sin(angle)
    if k == 0:
        return real, imag
    if 8 * k == n:
        return (real + imag) * c, (imag - real) * c
    if 8 * k == 3 * n:
        return (imag - real) * s, -(real + imag) * s
    return real * c + imag * s, imag * c - real * s


def real_fft(x):
    n = len(x)
    if n == 1:
        return [x[0]], [None]
    er, ei = real_fft(x[0::2])
    odr, odi = real_fft(x[1::2])
    half = n // 2
    re, im = [None] * (half + 1), [None] * (half + 1)
    re[0], re[half] = er[0] + odr[0], er[0] - odr[0]
    for k in range(1, half // 2 + 1):
        if 2 * k == half:
            re[k], im[k] = er[k], -odr[k]
            continue
        tr, ti = twisted(odr[k], odi[k], k, n)
        re[k], im[k] = er[k] + tr, ei[k] + ti
        re[half - k], im[half - k] = er[k] - tr, ti - ei[k]
    return re, im


def real_ifft(re, im):
    n = 2 * (len(re) - 1)
    if n == 0:
        return [re[0]]
    half = n // 2
    if n == 2:
        return [re[0] + re[1], re[0] - re[1]]
    quarter = half // 2
    er, ei = [None] * (quarter + 1), [None] * (quarter + 1)
    odr, odi = [None] * (quarter + 1), [None] * (quarter + 1)
    er[0], odr[0] = re[0] + re[half], re[0] - re[half]
    for k in range(1, quarter + 1):
        if k == quarter:
            er[k], odr[k] = 2.0 * re[k], -2.0 * im[k]
            continue
        sr, si = re[k] + re[half - k], im[k] - im[half - k]
        dr, di = re[k] - re[half - k], im[k] + im[half - k]
        er[k], ei[k] = sr, si
        odi[k], odr[k] = twisted(di, dr, k, n)
    even = real_ifft(er, ei)
    odd = real_ifft(odr, odi)
    out = [None] * n
    out[0::2], out[1::2] = even, odd
    return out


def filter_tables():
    b = np.arange(LANES)
    angle = 2.0 * np.pi * (np.outer(b, b) % LANES) / LANES
    c, s = np.cos(angle), np.sin(angle)
    forward = np.block([[c, -s], [s, c]])
    backward = forward.T / (RADIX * LANES)

    def split(w):
        hi = w.astype(np.float32).astype(ml_dtypes.bfloat16)
        lo = (w - hi.astype(np.float64)).astype(np.float32).astype(ml_dtypes.bfloat16)
        return hi, lo

    k1 = np.arange(40)[:, None]
    twist = 2.0 * np.pi * k1 * b[None, :] / (RADIX * LANES)
    return (
        *split(forward),
        *split(backward),
        np.cos(twist).astype(np.float32),
        np.sin(twist).astype(np.float32),
    )


def edge_kernel(th_ref, wi_ref, te_ref, tail_ref, head_ref, tile_ref, sems):
    rows = te_ref.shape[0]

    def copies(f):
        src = th_ref.at[f] if f < 2 else wi_ref.at[f - 2] if f < 6 else te_ref
        return [
            pltpu.make_async_copy(src.at[pl.ds(start, SUB)], tile_ref.at[i, f], sems.at[i, f])
            for i, start in enumerate((rows - SUB, 0))
        ]

    for f in range(7):
        for copy in copies(f):
            copy.start()
    for f in range(7):
        for i, copy in enumerate(copies(f)):
            copy.wait()
            out_ref, start = ((tail_ref, SUB - HALO), (head_ref, 0))[i]
            for s in range(SUB):
                out_ref[pl.ds(f * SUB + s, HALO, stride=7 * SUB), :] = tile_ref[
                    i, f, start : start + HALO, s * LANES : (s + 1) * LANES
                ]


def pack_kernel(outer, bands, lat_ref, th_hbm, wi_hbm, te_hbm, out_hbm, th_ref, wi_ref, te_ref, piece_ref, in_sems, sems):
    groups = piece_ref.shape[0]
    own = te_ref.shape[0] // groups
    tail = own - INNER

    def arrivals(g):
        rows = pl.ds(g * own, own)
        return (
            pltpu.make_async_copy(th_hbm.at[:, rows], th_ref.at[:, rows], in_sems.at[0, g]),
            pltpu.make_async_copy(wi_hbm.at[:, rows], wi_ref.at[:, rows], in_sems.at[1, g]),
            pltpu.make_async_copy(te_hbm.at[rows], te_ref.at[rows], in_sems.at[2, g]),
        )

    def departure(g):
        first = 0 if not outer or g > 0 else HALO
        last = INNER if not outer else HALO + tail + (HALO if g < groups - 1 else 0)
        rows = pl.ds(first * 7 * SUB, (last - first) * 7 * SUB)
        return pltpu.make_async_copy(piece_ref.at[g, rows], out_hbm.at[g, rows], sems.at[g])

    for g in range(groups):
        for copy in arrivals(g):
            copy.start()
    for copy in arrivals(0):
        copy.wait()
    for g in range(groups):
        if g < groups - 1:
            for copy in arrivals(g + 1):
                copy.wait()
        for f in range(7):
            src = th_ref.at[f] if f < 2 else wi_ref.at[f - 2] if f < 6 else te_ref

            def put(dst, start, count):
                for s in range(SUB):
                    piece_ref[g, pl.ds((dst * 7 + f) * SUB + s, count, stride=7 * SUB), :] = src[
                        pl.ds(start, count), s * LANES : (s + 1) * LANES
                    ]

            if not outer:
                for m in range(0, INNER, SUB):
                    put(m, g * own + m, min(SUB, INNER - m))
                continue
            if g > 0:
                put(0, g * own - HALO, HALO)
            put(HALO, g * own + INNER, tail)
            if g < groups - 1:
                put(HALO + tail, (g + 1) * own, HALO)
        if outer and g == groups - 1:

            @pl.when(lat_ref[0] == bands - 1)
            def _():
                for f in (4, 5):
                    at = pl.ds(((HALO + tail - 1) * 7 + f) * SUB, SUB)
                    piece_ref[g, at, :] = jnp.zeros((SUB, LANES), jnp.float32)

        departure(g).start()
    for g in range(groups):
        departure(g).wait()


def rim_kernel(south_ref, north_ref, packed_ref, out_ref, sems):
    groups, length = out_ref.shape[0], out_ref.shape[1]
    rim = HALO * 7 * SUB
    low = pltpu.make_async_copy(south_ref, out_ref.at[0, pl.ds(0, rim)], sems.at[0])
    high = pltpu.make_async_copy(north_ref, out_ref.at[groups - 1, pl.ds(length - rim, rim)], sems.at[1])
    low.start()
    high.start()
    low.wait()
    high.wait()


def unpack_kernel(low_ref, high_ref, th_hbm, wi_hbm, tile_ref, sems):
    groups = low_ref.shape[0]
    low_rows, high_rows = (r.shape[1] // (6 * SUB) for r in (low_ref, high_ref))
    own = low_rows + high_rows
    spans = (
        (low_ref, 0, HALO, low_rows),
        (high_ref, 0, 0, HALO),
        (high_ref, HALO, HALO + low_rows, high_rows - HALO),
    )

    def departure(f):
        dst = th_hbm.at[f] if f < 2 else wi_hbm.at[f - 2]
        return pltpu.make_async_copy(tile_ref.at[f], dst, sems.at[f])

    for f in range(6):
        for g in range(groups):
            for src, src_row, row, count in spans:
                for s in range(SUB):
                    tile_ref[f, pl.ds(g * own + row, count), s * LANES : (s + 1) * LANES] = src[
                        g, pl.ds((src_row * 6 + f) * SUB + s, count, stride=6 * SUB), :
                    ]
        departure(f).start()
    for f in range(6):
        departure(f).wait()


def stage_rows(height, outer):
    top = HALO + INNER
    if outer:
        return [((1 + k, HALO + k), (top - 1 - k, height - 2 - k)) for k in range(3)]
    return [((HALO + 1 + k, top - 2 - k),) for k in range(3)]


def step_kernel(outer, height, merid_step, step_size, coef, flags, *refs):
    if outer:
        x_low, x_high, s1_hbm, s2_hbm, *refs = refs
    else:
        x_low, *refs = refs
    cut_ref, wfh_ref, wfl_ref, wbh_ref, wbl_ref, twc_ref, tws_ref, *refs = refs
    out_hbm, *refs = refs
    if not outer:
        s1_hbm, s2_hbm, *refs = refs
    x_ref, s1_ref, s2_ref, out_ref, t_ref, in_sems, out_sems, edge_sems, *refs = refs
    e_ref, z_ref, uu_ref, vv_ref, *y_refs = refs
    chunks = x_ref.shape[0]
    ranges = stage_rows(height, outer)
    top = HALO + INNER
    lane = lax.broadcasted_iota(jnp.int32, (SUB, LANES), 1)
    sub = lax.broadcasted_iota(jnp.int32, (SUB, LANES), 0)
    last_lane, first_lane = lane == LANES - 1, lane == 0
    last_sub, first_sub = sub == SUB - 1, sub == 0
    dy_inv = 1.0 / merid_step

    def east(xs):
        y = [pltpu.roll(x, LANES - 1, 1) for x in xs]
        r = [pltpu.roll(v, SUB - 1, 0) for v in y]
        return [
            jnp.where(last_lane, jnp.where(last_sub, r[(d + 1) % chunks], r[d]), y[d])
            for d in range(chunks)
        ]

    def west(xs):
        y = [pltpu.roll(x, 1, 1) for x in xs]
        r = [pltpu.roll(v, 1, 0) for v in y]
        return [
            jnp.where(first_lane, jnp.where(first_sub, r[d - 1], r[d]), y[d]) for d in range(chunks)
        ]

    def x_copy(i, src, src_row, row, count):
        return pltpu.make_async_copy(
            src.at[:, pl.ds(src_row * 7, count * 7)], x_ref.at[:, pl.ds(row * 7, count * 7)], in_sems.at[i]
        )

    if outer:
        arrivals = [
            [x_copy(0, x_high, 0, 0, HALO), x_copy(1, x_low, 0, HALO, HALO)],
            [x_copy(2, x_low, INNER - HALO, top - HALO, HALO), x_copy(3, x_high, HALO, top, height - top)],
        ]
        out_edges = (0, HALO, height - 2 * HALO - (INNER - 6))
    else:
        bounds = (0, INNER // 3, 2 * INNER // 3, INNER)
        arrivals = [
            [x_copy(i, x_low, lo, HALO + lo, hi - lo)] for i, (lo, hi) in enumerate(zip(bounds, bounds[1:]))
        ]
        out_edges = (0, (INNER - 6) // 2, INNER - 6)

    def departure(i):
        rows = pl.ds(out_edges[i] * 6, (out_edges[i + 1] - out_edges[i]) * 6)
        return pltpu.make_async_copy(out_ref.at[:, rows], out_hbm.at[:, rows], out_sems.at[i])

    def edges(index):
        hbm, ref = ((s1_hbm, s1_ref), (s2_hbm, s2_ref))[index]
        copies = []
        for i, row in enumerate((HALO + 1 + index, top - 3 - index)):
            src, dst = hbm.at[:, pl.ds(i * 12, 12)], ref.at[:, pl.ds(row * 6, 12)]
            src, dst = (src, dst) if outer else (dst, src)
            copies.append(pltpu.make_async_copy(src, dst, edge_sems.at[index, i]))
        return copies

    for copy in sum(arrivals, []):
        copy.start()
    if outer:
        for copy in edges(0) + edges(1):
            copy.start()

    def stage(src, dst, index, fraction):
        fields = 7 if index == 0 else 6
        final = index == 2
        count = sum(hi - lo + 1 for lo, hi in ranges[index])

        def get(f, r):
            return [src[d, r * fields + f] for d in range(chunks)]

        def terrain(r):
            return [x_ref[d, r * 7 + 6] for d in range(chunks)]

        def corners(in_lo, in_hi, r, carry):
            rn = jnp.minimum(r + 1, in_hi)
            rs = jnp.maximum(r - 1, in_lo)
            c_half, cn_half = coef[0, r] * dy_inv, coef[0, rn] * dy_inv
            e_inv, sine = coef[2, r], coef[3, r]
            h0, h1, ground = get(0, r), get(1, r), terrain(r)
            base = [a + b for a, b in zip(h1, ground)]
            for k in range(2):
                u, v = get(2 + k, r), get(4 + k, r)
                uw, ve = west(u), east(v)
                un, vs = get(2 + k, rn), get(4 + k, rs)
                for d in range(chunks):
                    at = (r * 2 + k) * chunks + d
                    uu_ref[at] = u[d] + uw[d]
                    vv_ref[at] = v[d] + ve[d]
                    kin = 0.25 * (u[d] * u[d] + uw[d] * uw[d] + (v[d] * v[d] + vs[d] * vs[d]))
                    e_ref[at] = kin + (base[d] + (h0[d] if k == 0 else DENSITY_RATIO * h0[d]))
                    curl = (ve[d] - v[d]) - (un[d] * cn_half - u[d] * c_half)
                    z_ref[at] = sine + curl * e_inv
            return carry

        def tendencies(shift, r, carry):
            c_inv = coef[1, r]
            fn, fs = coef[4, r] * (0.5 * dy_inv), coef[4, r - 1] * (0.5 * dy_inv)
            live = coef[5, r]
            for k in range(2):

                def face(ref, row):
                    return [ref[(row * 2 + k) * chunks + d] for d in range(chunks)]

                def put(f, d, value):
                    start = (d * TILE_ROWS + (r - shift) * 6 + f) * SUB
                    t_ref[pl.ds(pl.multiple_of(start, SUB), SUB), :] = value

                h, hn, hs = get(k, r), get(k, r + 1), get(k, r - 1)
                u, v, vs = get(2 + k, r), get(4 + k, r), get(4 + k, r - 1)
                he = east(h)
                fx = [0.5 * (h[d] + he[d]) * u[d] for d in range(chunks)]
                fxw = west(fx)
                for d in range(chunks):
                    north = (h[d] + hn[d]) * (v[d] * fn) - (h[d] + hs[d]) * (vs[d] * fs)
                    put(k, d, ((fxw[d] - fx[d]) - north) * c_inv)
                z, zs, ec = face(z_ref, r), face(z_ref, r - 1), face(e_ref, r)
                vv, vvs = face(vv_ref, r), face(vv_ref, r - 1)
                ee = east(ec)
                for d in range(chunks):
                    turn = (0.125 * (z[d] + zs[d])) * (vv[d] + vvs[d])
                    put(2 + k, d, turn - (ee[d] - ec[d]) * c_inv)
                en, uu, uun = face(e_ref, r + 1), face(uu_ref, r), face(uu_ref, r + 1)
                zw = west(z)
                for d in range(chunks):
                    turn = (0.125 * (z[d] + zw[d])) * (uu[d] + uun[d])
                    put(4 + k, d, live * (dy_inv * (ec[d] - en[d]) - turn))
            return carry

        if index > 0 and outer:
            for copy in edges(index - 1):
                copy.wait()
        base = 0
        for i, (lo, hi) in enumerate(ranges[index]):
            calc = functools.partial(corners, lo - 1, hi + 1)
            if index > 0:
                lax.fori_loop(lo - 1, hi + 2, calc, 0)
            elif outer:
                for copy in arrivals[i]:
                    copy.wait()
                lax.fori_loop(lo - 1, hi + 2, calc, 0)
            else:
                first = lo - 1
                for j, (copy,) in enumerate(arrivals):
                    copy.wait()
                    last = HALO + bounds[j + 1] - (1 if j < 2 else 0)
                    lax.fori_loop(first, last, calc, 0)
                    first = last
            lax.fori_loop(lo, hi + 1, functools.partial(tendencies, lo - base), 0)
            base += hi - lo + 1

        total = -(-6 * count // PAIR)
        units = 2 if total == 4 else 3

        def circle_filter(p, carry):
            wave = lax.broadcasted_iota(jnp.int32, (PAIR, 2 * LANES), 1)
            wave = RADIX * jnp.where(wave >= LANES, wave - LANES, wave)

            def place(unit, a, half):
                d, s = a // SUB, a % SUB
                start = (d * TILE_ROWS + (p * units + unit) * PAIR + half * SUB) * SUB + s
                return pl.ds(start, SUB, stride=SUB)

            def cut_of(unit):
                at = pl.multiple_of((p * units + unit) * PAIR, PAIR)
                return cut_ref[3 * outer + index, pl.ds(at, PAIR), :]

            def analyse(unit, half):
                re, im = real_fft([t_ref[place(unit, a, half), :] for a in range(RADIX)])
                for k in range(HALF + 1):
                    c, s = twc_ref[k : k + 1, :], tws_ref[k : k + 1, :]
                    if k == 0:
                        yr, yi = re[k], jnp.zeros_like(re[k])
                    elif im[k] is None:
                        yr, yi = re[k] * c, -(re[k] * s)
                    else:
                        yr, yi = re[k] * c + im[k] * s, im[k] * c - re[k] * s
                    at = pl.ds((k * 2 + half) * SUB, SUB)
                    y_refs[unit][at, 0:LANES] = yr
                    y_refs[unit][at, LANES : 2 * LANES] = yi

            def product(y, whi, wlo):
                n = y.shape[0]
                hi_part = y.astype(jnp.bfloat16)
                lo_part = (y - hi_part.astype(jnp.float32)).astype(jnp.bfloat16)
                dot = functools.partial(jnp.dot, preferred_element_type=jnp.float32)
                both = dot(jnp.concatenate([hi_part, lo_part], axis=0), whi)
                return both[:n] + both[n:] + dot(hi_part, wlo)

            def mask(unit, start):
                cut = cut_of(unit)
                cut2 = jnp.concatenate([cut, cut], axis=1)
                rows = slice(start * PAIR, (start + BLOCK) * PAIR)
                spec = product(y_refs[unit][rows, :], wfh_ref[...], wfl_ref[...])
                keep = []
                for k in range(start, start + BLOCK):
                    folded = jnp.minimum(wave + k, RADIX * LANES - k - wave)
                    keep.append(folded < cut2)
                spec = jnp.where(jnp.concatenate(keep, axis=0), spec, 0.0)
                y_refs[unit][rows, :] = product(spec, wbh_ref[...], wbl_ref[...])

            def synthesise(unit, half):
                re, im = [], []
                for k in range(HALF + 1):
                    c, s = twc_ref[k : k + 1, :], tws_ref[k : k + 1, :]
                    at = pl.ds((k * 2 + half) * SUB, SUB)
                    yr = y_refs[unit][at, 0:LANES]
                    if k == 0:
                        re.append(yr)
                        im.append(None)
                        continue
                    yi = y_refs[unit][at, LANES : 2 * LANES]
                    re.append(yr * c - yi * s)
                    im.append(None if k == HALF else yr * s + yi * c)
                circles = real_ifft(re, im)
                polar = cut_of(unit)[half * SUB : (half + 1) * SUB] < UNCUT
                for a in range(RADIX):
                    at = place(unit, a, half)
                    t_ref[at, :] = jnp.where(polar, circles[a], t_ref[at, :])

            for unit in range(units):
                for half in range(2):
                    analyse(unit, half)
            for start in range(0, HALF + 1, BLOCK):
                for unit in range(units):
                    mask(unit, start)
            for unit in range(units):
                for half in range(2):
                    synthesise(unit, half)
            return carry

        @pl.when(flags[3 * outer + index] > 0)
        def _():
            lax.fori_loop(0, -(-total // units), circle_filter, 0)

        def update(shift, r, carry):
            inside = coef[6, r]
            for f in range(6):
                for d in range(chunks):
                    start = (d * TILE_ROWS + (r - shift) * 6 + f) * SUB
                    change = t_ref[pl.ds(pl.multiple_of(start, SUB), SUB), :]
                    value = inside * (x_ref[d, r * 7 + f] + (fraction * step_size) * change)
                    if final:
                        out_ref[d, (r - shift) * 6 + f] = value
                    else:
                        dst[d, r * 6 + f] = value
            return carry

        spans = ranges[index]
        if final and not outer:
            (lo, hi), middle = spans[0], spans[0][0] + out_edges[1]
            spans = ((lo, middle - 1), (middle, hi))
        base = 0
        for i, (lo, hi) in enumerate(spans):
            lax.fori_loop(lo, hi + 1, functools.partial(update, lo - base), 0)
            base += hi - lo + 1
            if final:
                departure(i).start()
        if not final and not outer:
            for copy in edges(index):
                copy.start()

    stage(x_ref, s1_ref, 0, 1.0 / 3.0)
    stage(s1_ref, s2_ref, 1, 0.5)
    stage(s2_ref, None, 2, 1.0)
    for i in range(2):
        departure(i).wait()
        if not outer:
            for copy in edges(i):
                copy.wait()


def row_tables(cutoffs, row_start, height, total_rows, polar):
    row_ids = row_start - HALO + jnp.arange(height, dtype=jnp.int32)
    spacing = math.pi / total_rows
    centre_lat = -0.5 * math.pi + (row_ids.astype(jnp.float32) + 0.5) * spacing
    face_lat = -0.5 * math.pi + (row_ids.astype(jnp.float32) + 1.0) * spacing
    inside = jnp.where((row_ids >= 0) & (row_ids < total_rows), 1.0, 0.0).astype(jnp.float32)
    live = jnp.where((row_ids >= 0) & (row_ids < total_rows - 1), 1.0, 0.0).astype(jnp.float32)
    centre_cos = jnp.cos(centre_lat)
    face_cos = jnp.cos(face_lat) * live
    face_inverse = live / (face_cos + (1.0 - live))
    coef = jnp.stack(
        [centre_cos, 1.0 / centre_cos, face_inverse, jnp.sin(face_lat), face_cos, live, inside]
    )
    capped = ((row_ids >= 0) & (row_ids < polar)) | (
        (row_ids >= total_rows - polar) & (row_ids < total_rows)
    )
    position = jnp.where(row_ids < polar, row_ids, row_ids - (total_rows - 2 * polar))
    table_ids = jnp.arange(2 * polar, dtype=jnp.int32)
    cut = jnp.sum(
        jnp.where(position[:, None] == table_ids[None, :], cutoffs[None, :], 0), axis=1, dtype=jnp.int32
    )
    cut = jnp.where(capped, cut, UNCUT)
    stages = []
    for outer in (False, True):
        for spans in stage_rows(height, outer):
            rows = jnp.repeat(jnp.concatenate([cut[lo : hi + 1] for lo, hi in spans]), 6)
            stages.append(jnp.pad(rows, (0, TILE_ROWS - rows.shape[0]), constant_values=UNCUT))
    cuts = jnp.stack(stages)
    flags = jnp.any(cuts < UNCUT, axis=1).astype(jnp.int32)
    return coef, flags, jnp.broadcast_to(cuts[:, :, None], (6, TILE_ROWS, LANES))


def body(thickness, winds, terrain, cutoffs):
    row_count, col_count = thickness.shape[1], thickness.shape[2]
    bands, sectors = lax.axis_size("lat"), lax.axis_size("lon")
    total_rows, circle = row_count * bands, col_count * sectors
    polar = (total_rows + 2) // 6
    own = row_count // sectors
    height = own + 2 * HALO
    merid_step = circle / (2.0 * total_rows)
    step_size = 0.1 * min(1.0, merid_step)
    lat = lax.axis_index("lat")
    flat = winds.reshape(4, row_count, col_count)

    vmem = pl.BlockSpec(memory_space=pltpu.VMEM)
    smem = pl.BlockSpec(memory_space=pltpu.SMEM)
    hbm = pl.BlockSpec(memory_space=pltpu.HBM)
    rim = jax.ShapeDtypeStruct((HALO * 7 * SUB, LANES), jnp.float32)
    tail, head = pl.pallas_call(
        edge_kernel,
        out_shape=(rim, rim),
        in_specs=[hbm] * 3,
        out_specs=(vmem, vmem),
        scratch_shapes=[
            pltpu.VMEM((2, 7, SUB, col_count), jnp.float32),
            pltpu.SemaphoreType.DMA((2, 7)),
        ],
        name="edge",
    )(thickness, flat, terrain)
    south = lax.ppermute(tail, "lat", [(i, i + 1) for i in range(bands - 1)])
    north = lax.ppermute(head, "lat", [(i + 1, i) for i in range(bands - 1)])

    def piece(rows, fields):
        return jax.ShapeDtypeStruct((sectors, rows * fields * SUB, LANES), jnp.float32)

    def pack(outer):
        out = piece(height - INNER if outer else INNER, 7)
        return pl.pallas_call(
            functools.partial(pack_kernel, outer, bands),
            out_shape=out,
            in_specs=[smem] + [hbm] * 3,
            out_specs=hbm,
            scratch_shapes=[
                pltpu.VMEM(thickness.shape, jnp.float32),
                pltpu.VMEM(flat.shape, jnp.float32),
                pltpu.VMEM(terrain.shape, jnp.float32),
                pltpu.VMEM(out.shape, jnp.float32),
                pltpu.SemaphoreType.DMA((3, sectors)),
                pltpu.SemaphoreType.DMA((sectors,)),
            ],
            compiler_params=pltpu.CompilerParams(vmem_limit_bytes=56 << 20),
            cost_estimate=pl.CostEstimate(flops=0, bytes_accessed=12 << 20, transcendentals=0),
            name="pack_outer" if outer else "pack_inner",
        )(lat.reshape(1).astype(jnp.int32), thickness, flat, terrain)

    packed_low = pack(False)
    packed_high = pack(True)
    packed_high = pl.pallas_call(
        rim_kernel,
        out_shape=jax.ShapeDtypeStruct(packed_high.shape, jnp.float32),
        in_specs=[vmem, vmem, hbm],
        out_specs=hbm,
        scratch_shapes=[pltpu.SemaphoreType.DMA((2,))],
        input_output_aliases={2: 0},
        name="rim",
    )(south, north, packed_high)
    row_start = lat * row_count + lax.axis_index("lon") * own
    coef, flags, cuts = row_tables(cutoffs, row_start, height, total_rows, polar)
    packed_high, coef, flags, cuts = lax.optimization_barrier((packed_high, coef, flags, cuts))
    circles_low = lax.all_to_all(packed_low, "lon", 0, 0)
    circles_high = lax.all_to_all(packed_high, "lon", 0, 0)

    tables = [jnp.asarray(t) for t in filter_tables()]
    edges = jax.ShapeDtypeStruct((sectors, 24, SUB, LANES), jnp.float32)

    def step(outer, states, saved):
        rows = sum(hi - lo + 1 for lo, hi in stage_rows(height, outer)[2])
        out = jax.ShapeDtypeStruct((sectors, 6 * rows, SUB, LANES), jnp.float32)
        states = [x.reshape(sectors, -1, SUB, LANES) for x in states]
        return pl.pallas_call(
            functools.partial(step_kernel, outer, height, merid_step, step_size),
            out_shape=out if outer else (out, edges, edges),
            in_specs=[smem, smem] + [hbm] * len(states + saved) + [vmem] * 7,
            out_specs=hbm if outer else (hbm, hbm, hbm),
            scratch_shapes=[
                pltpu.VMEM((sectors, 7 * height, SUB, LANES), jnp.float32),
                pltpu.VMEM((sectors, 6 * height, SUB, LANES), jnp.float32),
                pltpu.VMEM((sectors, 6 * height, SUB, LANES), jnp.float32),
                pltpu.VMEM(out.shape, jnp.float32),
                pltpu.VMEM((sectors * TILE_ROWS * SUB, LANES), jnp.float32),
                pltpu.SemaphoreType.DMA((4,)),
                pltpu.SemaphoreType.DMA((2,)),
                pltpu.SemaphoreType.DMA((2, 2)),
            ]
            + [pltpu.VMEM((height * 2 * sectors, SUB, LANES), jnp.float32)] * 4
            + [pltpu.VMEM(((HALF + 1) * PAIR, 2 * LANES), jnp.float32)] * UNITS,
            compiler_params=pltpu.CompilerParams(vmem_limit_bytes=51 << 20),
            cost_estimate=pl.CostEstimate(flops=0, bytes_accessed=64 << 20, transcendentals=0),
            name="step_outer" if outer else "step_inner",
        )(coef, flags, *states, *saved, cuts, *tables)

    new_low, *saved = step(False, [circles_low], [])
    returned_low = lax.all_to_all(new_low.reshape(sectors, -1, LANES), "lon", 0, 0)
    new_high = step(True, [circles_low, circles_high], saved)
    returned_low, new_high = lax.optimization_barrier((returned_low, new_high))
    returned_high = lax.all_to_all(new_high.reshape(sectors, -1, LANES), "lon", 0, 0)

    new_thickness, new_winds = pl.pallas_call(
        unpack_kernel,
        out_shape=(
            jax.ShapeDtypeStruct(thickness.shape, jnp.float32),
            jax.ShapeDtypeStruct(flat.shape, jnp.float32),
        ),
        in_specs=[vmem, vmem],
        out_specs=(hbm, hbm),
        scratch_shapes=[
            pltpu.VMEM((6, row_count, col_count), jnp.float32),
            pltpu.SemaphoreType.DMA((6,)),
        ],
        compiler_params=pltpu.CompilerParams(vmem_limit_bytes=40 << 20),
        name="unpack",
    )(returned_low, returned_high)
    return new_thickness, new_winds.reshape(winds.shape)


def solution(mesh):
    in_specs = (P(None, "lat", "lon"), P(None, None, "lat", "lon"), P("lat", "lon"), P())
    out_specs = (P(None, "lat", "lon"), P(None, None, "lat", "lon"))
    return jax.shard_map(body, mesh=mesh, in_specs=in_specs, out_specs=out_specs, check_vma=False)
```

```python
import functools
import math

import jax
import jax.numpy as jnp
import ml_dtypes
import numpy as np
from jax import lax
from jax.experimental import pallas as pl
from jax.experimental.pallas import tpu as pltpu
from jax.sharding import PartitionSpec as P

DENSITY_RATIO = 0.9
HALO = 3
SUB = 8
LANES = 128
RADIX = 64
HALF = RADIX // 2
UNCUT = 1 << 20
TILE_ROWS = 96
PAIR = 16
UNITS = 3
BLOCK = 11
INNER = 14


def twisted(real, imag, k, n):
    angle = 2.0 * math.pi * k / n
    c, s = math.cos(angle), math.sin(angle)
    if k == 0:
        return real, imag
    if 8 * k == n:
        return (real + imag) * c, (imag - real) * c
    if 8 * k == 3 * n:
        return (imag - real) * s, -(real + imag) * s
    return real * c + imag * s, imag * c - real * s


def real_fft(x):
    n = len(x)
    if n == 1:
        return [x[0]], [None]
    er, ei = real_fft(x[0::2])
    odr, odi = real_fft(x[1::2])
    half = n // 2
    re, im = [None] * (half + 1), [None] * (half + 1)
    re[0], re[half] = er[0] + odr[0], er[0] - odr[0]
    for k in range(1, half // 2 + 1):
        if 2 * k == half:
            re[k], im[k] = er[k], -odr[k]
            continue
        tr, ti = twisted(odr[k], odi[k], k, n)
        re[k], im[k] = er[k] + tr, ei[k] + ti
        re[half - k], im[half - k] = er[k] - tr, ti - ei[k]
    return re, im


def real_ifft(re, im):
    n = 2 * (len(re) - 1)
    if n == 0:
        return [re[0]]
    half = n // 2
    if n == 2:
        return [re[0] + re[1], re[0] - re[1]]
    quarter = half // 2
    er, ei = [None] * (quarter + 1), [None] * (quarter + 1)
    odr, odi = [None] * (quarter + 1), [None] * (quarter + 1)
    er[0], odr[0] = re[0] + re[half], re[0] - re[half]
    for k in range(1, quarter + 1):
        if k == quarter:
            er[k], odr[k] = 2.0 * re[k], -2.0 * im[k]
            continue
        sr, si = re[k] + re[half - k], im[k] - im[half - k]
        dr, di = re[k] - re[half - k], im[k] + im[half - k]
        er[k], ei[k] = sr, si
        odi[k], odr[k] = twisted(di, dr, k, n)
    even = real_ifft(er, ei)
    odd = real_ifft(odr, odi)
    out = [None] * n
    out[0::2], out[1::2] = even, odd
    return out


def filter_tables():
    b = np.arange(LANES)
    angle = 2.0 * np.pi * (np.outer(b, b) % LANES) / LANES
    c, s = np.cos(angle), np.sin(angle)
    forward = np.block([[c, -s], [s, c]])
    backward = forward.T / (RADIX * LANES)

    def split(w):
        hi = w.astype(np.float32).astype(ml_dtypes.bfloat16)
        lo = (w - hi.astype(np.float64)).astype(np.float32).astype(ml_dtypes.bfloat16)
        return hi, lo

    k1 = np.arange(40)[:, None]
    twist = 2.0 * np.pi * k1 * b[None, :] / (RADIX * LANES)
    return (
        *split(forward),
        *split(backward),
        np.cos(twist).astype(np.float32),
        np.sin(twist).astype(np.float32),
    )


def edge_kernel(th_ref, wi_ref, te_ref, tail_ref, head_ref, tile_ref, sems):
    rows = te_ref.shape[0]

    def copies(f):
        src = th_ref.at[f] if f < 2 else wi_ref.at[f - 2] if f < 6 else te_ref
        return [
            pltpu.make_async_copy(src.at[pl.ds(start, SUB)], tile_ref.at[i, f], sems.at[i, f])
            for i, start in enumerate((rows - SUB, 0))
        ]

    for f in range(7):
        for copy in copies(f):
            copy.start()
    for f in range(7):
        for i, copy in enumerate(copies(f)):
            copy.wait()
            out_ref, start = ((tail_ref, SUB - HALO), (head_ref, 0))[i]
            for s in range(SUB):
                out_ref[pl.ds(f * SUB + s, HALO, stride=7 * SUB), :] = tile_ref[
                    i, f, start : start + HALO, s * LANES : (s + 1) * LANES
                ]


def pack_kernel(outer, bands, lat_ref, th_hbm, wi_hbm, te_hbm, out_hbm, th_ref, wi_ref, te_ref, piece_ref, in_sems, sems):
    groups = piece_ref.shape[0]
    own = te_ref.shape[0] // groups
    tail = own - INNER

    def arrivals(g):
        rows = pl.ds(g * own, own)
        return (
            pltpu.make_async_copy(th_hbm.at[:, rows], th_ref.at[:, rows], in_sems.at[0, g]),
            pltpu.make_async_copy(wi_hbm.at[:, rows], wi_ref.at[:, rows], in_sems.at[1, g]),
            pltpu.make_async_copy(te_hbm.at[rows], te_ref.at[rows], in_sems.at[2, g]),
        )

    def departure(g):
        first = 0 if not outer or g > 0 else HALO
        last = INNER if not outer else HALO + tail + (HALO if g < groups - 1 else 0)
        rows = pl.ds(first * 7 * SUB, (last - first) * 7 * SUB)
        return pltpu.make_async_copy(piece_ref.at[g, rows], out_hbm.at[g, rows], sems.at[g])

    for g in range(groups):
        for copy in arrivals(g):
            copy.start()
    for copy in arrivals(0):
        copy.wait()
    for g in range(groups):
        if g < groups - 1:
            for copy in arrivals(g + 1):
                copy.wait()
        for f in range(7):
            src = th_ref.at[f] if f < 2 else wi_ref.at[f - 2] if f < 6 else te_ref

            def put(dst, start, count):
                for s in range(SUB):
                    piece_ref[g, pl.ds((dst * 7 + f) * SUB + s, count, stride=7 * SUB), :] = src[
                        pl.ds(start, count), s * LANES : (s + 1) * LANES
                    ]

            if not outer:
                for m in range(0, INNER, SUB):
                    put(m, g * own + m, min(SUB, INNER - m))
                continue
            if g > 0:
                put(0, g * own - HALO, HALO)
            put(HALO, g * own + INNER, tail)
            if g < groups - 1:
                put(HALO + tail, (g + 1) * own, HALO)
        if outer and g == groups - 1:

            @pl.when(lat_ref[0] == bands - 1)
            def _():
                for f in (4, 5):
                    at = pl.ds(((HALO + tail - 1) * 7 + f) * SUB, SUB)
                    piece_ref[g, at, :] = jnp.zeros((SUB, LANES), jnp.float32)

        departure(g).start()
    for g in range(groups):
        departure(g).wait()


def rim_kernel(south_ref, north_ref, packed_ref, out_ref, sems):
    groups, length = out_ref.shape[0], out_ref.shape[1]
    rim = HALO * 7 * SUB
    low = pltpu.make_async_copy(south_ref, out_ref.at[0, pl.ds(0, rim)], sems.at[0])
    high = pltpu.make_async_copy(north_ref, out_ref.at[groups - 1, pl.ds(length - rim, rim)], sems.at[1])
    low.start()
    high.start()
    low.wait()
    high.wait()


def unpack_kernel(low_ref, high_ref, th_hbm, wi_hbm, tile_ref, sems):
    groups = low_ref.shape[0]
    low_rows, high_rows = (r.shape[1] // (6 * SUB) for r in (low_ref, high_ref))
    own = low_rows + high_rows
    spans = (
        (low_ref, 0, HALO, low_rows),
        (high_ref, 0, 0, HALO),
        (high_ref, HALO, HALO + low_rows, high_rows - HALO),
    )

    def departure(f):
        dst = th_hbm.at[f] if f < 2 else wi_hbm.at[f - 2]
        return pltpu.make_async_copy(tile_ref.at[f], dst, sems.at[f])

    for f in range(6):
        for g in range(groups):
            for src, src_row, row, count in spans:
                for s in range(SUB):
                    tile_ref[f, pl.ds(g * own + row, count), s * LANES : (s + 1) * LANES] = src[
                        g, pl.ds((src_row * 6 + f) * SUB + s, count, stride=6 * SUB), :
                    ]
        departure(f).start()
    for f in range(6):
        departure(f).wait()


def stage_rows(height, outer):
    top = HALO + INNER
    if outer:
        return [((1 + k, HALO + k), (top - 1 - k, height - 2 - k)) for k in range(3)]
    return [((HALO + 1 + k, top - 2 - k),) for k in range(3)]


def step_kernel(outer, height, merid_step, step_size, coef, flags, *refs):
    if outer:
        x_low, x_high, s1_hbm, s2_hbm, *refs = refs
    else:
        x_low, *refs = refs
    cut_ref, wfh_ref, wfl_ref, wbh_ref, wbl_ref, twc_ref, tws_ref, *refs = refs
    out_hbm, *refs = refs
    if not outer:
        s1_hbm, s2_hbm, *refs = refs
    x_ref, s1_ref, s2_ref, out_ref, t_ref, in_sems, out_sems, edge_sems, *refs = refs
    e_ref, z_ref, uu_ref, vv_ref, *y_refs = refs
    chunks = x_ref.shape[0]
    ranges = stage_rows(height, outer)
    top = HALO + INNER
    lane = lax.broadcasted_iota(jnp.int32, (SUB, LANES), 1)
    sub = lax.broadcasted_iota(jnp.int32, (SUB, LANES), 0)
    last_lane, first_lane = lane == LANES - 1, lane == 0
    last_sub, first_sub = sub == SUB - 1, sub == 0
    dy_inv = 1.0 / merid_step

    def east(xs):
        y = [pltpu.roll(x, LANES - 1, 1) for x in xs]
        r = [pltpu.roll(v, SUB - 1, 0) for v in y]
        return [
            jnp.where(last_lane, jnp.where(last_sub, r[(d + 1) % chunks], r[d]), y[d])
            for d in range(chunks)
        ]

    def west(xs):
        y = [pltpu.roll(x, 1, 1) for x in xs]
        r = [pltpu.roll(v, 1, 0) for v in y]
        return [
            jnp.where(first_lane, jnp.where(first_sub, r[d - 1], r[d]), y[d]) for d in range(chunks)
        ]

    def x_copy(i, src, src_row, row, count):
        return pltpu.make_async_copy(
            src.at[:, pl.ds(src_row * 7, count * 7)], x_ref.at[:, pl.ds(row * 7, count * 7)], in_sems.at[i]
        )

    if outer:
        arrivals = [
            [x_copy(0, x_high, 0, 0, HALO), x_copy(1, x_low, 0, HALO, HALO)],
            [x_copy(2, x_low, INNER - HALO, top - HALO, HALO), x_copy(3, x_high, HALO, top, height - top)],
        ]
        out_edges = (0, HALO, height - 2 * HALO - (INNER - 6))
    else:
        bounds = (0, INNER // 3, 2 * INNER // 3, INNER)
        arrivals = [
            [x_copy(i, x_low, lo, HALO + lo, hi - lo)] for i, (lo, hi) in enumerate(zip(bounds, bounds[1:]))
        ]
        out_edges = (0, (INNER - 6) // 2, INNER - 6)

    def departure(i):
        rows = pl.ds(out_edges[i] * 6, (out_edges[i + 1] - out_edges[i]) * 6)
        return pltpu.make_async_copy(out_ref.at[:, rows], out_hbm.at[:, rows], out_sems.at[i])

    def edges(index):
        hbm, ref = ((s1_hbm, s1_ref), (s2_hbm, s2_ref))[index]
        copies = []
        for i, row in enumerate((HALO + 1 + index, top - 3 - index)):
            src, dst = hbm.at[:, pl.ds(i * 12, 12)], ref.at[:, pl.ds(row * 6, 12)]
            src, dst = (src, dst) if outer else (dst, src)
            copies.append(pltpu.make_async_copy(src, dst, edge_sems.at[index, i]))
        return copies

    for copy in sum(arrivals, []):
        copy.start()
    if outer:
        for copy in edges(0) + edges(1):
            copy.start()

    def stage(src, dst, index, fraction):
        fields = 7 if index == 0 else 6
        final = index == 2
        count = sum(hi - lo + 1 for lo, hi in ranges[index])

        def get(f, r):
            return [src[d, r * fields + f] for d in range(chunks)]

        def terrain(r):
            return [x_ref[d, r * 7 + 6] for d in range(chunks)]

        def corners(in_lo, in_hi, r, carry):
            rn = jnp.minimum(r + 1, in_hi)
            rs = jnp.maximum(r - 1, in_lo)
            c_half, cn_half = coef[0, r] * dy_inv, coef[0, rn] * dy_inv
            e_inv, sine = coef[2, r], coef[3, r]
            h0, h1, ground = get(0, r), get(1, r), terrain(r)
            base = [a + b for a, b in zip(h1, ground)]
            for k in range(2):
                u, v = get(2 + k, r), get(4 + k, r)
                uw, ve = west(u), east(v)
                un, vs = get(2 + k, rn), get(4 + k, rs)
                for d in range(chunks):
                    at = (r * 2 + k) * chunks + d
                    uu_ref[at] = u[d] + uw[d]
                    vv_ref[at] = v[d] + ve[d]
                    kin = 0.25 * (u[d] * u[d] + uw[d] * uw[d] + (v[d] * v[d] + vs[d] * vs[d]))
                    e_ref[at] = kin + (base[d] + (h0[d] if k == 0 else DENSITY_RATIO * h0[d]))
                    curl = (ve[d] - v[d]) - (un[d] * cn_half - u[d] * c_half)
                    z_ref[at] = sine + curl * e_inv
            return carry

        def tendencies(shift, r, carry):
            c_inv = coef[1, r]
            fn, fs = coef[4, r] * (0.5 * dy_inv), coef[4, r - 1] * (0.5 * dy_inv)
            live = coef[5, r]
            for k in range(2):

                def face(ref, row):
                    return [ref[(row * 2 + k) * chunks + d] for d in range(chunks)]

                def put(f, d, value):
                    start = (d * TILE_ROWS + (r - shift) * 6 + f) * SUB
                    t_ref[pl.ds(pl.multiple_of(start, SUB), SUB), :] = value

                h, hn, hs = get(k, r), get(k, r + 1), get(k, r - 1)
                u, v, vs = get(2 + k, r), get(4 + k, r), get(4 + k, r - 1)
                he = east(h)
                fx = [0.5 * (h[d] + he[d]) * u[d] for d in range(chunks)]
                fxw = west(fx)
                for d in range(chunks):
                    north = (h[d] + hn[d]) * (v[d] * fn) - (h[d] + hs[d]) * (vs[d] * fs)
                    put(k, d, ((fxw[d] - fx[d]) - north) * c_inv)
                z, zs, ec = face(z_ref, r), face(z_ref, r - 1), face(e_ref, r)
                vv, vvs = face(vv_ref, r), face(vv_ref, r - 1)
                ee = east(ec)
                for d in range(chunks):
                    turn = (0.125 * (z[d] + zs[d])) * (vv[d] + vvs[d])
                    put(2 + k, d, turn - (ee[d] - ec[d]) * c_inv)
                en, uu, uun = face(e_ref, r + 1), face(uu_ref, r), face(uu_ref, r + 1)
                zw = west(z)
                for d in range(chunks):
                    turn = (0.125 * (z[d] + zw[d])) * (uu[d] + uun[d])
                    put(4 + k, d, live * (dy_inv * (ec[d] - en[d]) - turn))
            return carry

        if index > 0 and outer:
            for copy in edges(index - 1):
                copy.wait()
        base = 0
        for i, (lo, hi) in enumerate(ranges[index]):
            calc = functools.partial(corners, lo - 1, hi + 1)
            if index > 0:
                lax.fori_loop(lo - 1, hi + 2, calc, 0)
            elif outer:
                for copy in arrivals[i]:
                    copy.wait()
                lax.fori_loop(lo - 1, hi + 2, calc, 0)
            else:
                first = lo - 1
                for j, (copy,) in enumerate(arrivals):
                    copy.wait()
                    last = HALO + bounds[j + 1] - (1 if j < 2 else 0)
                    lax.fori_loop(first, last, calc, 0)
                    first = last
            lax.fori_loop(lo, hi + 1, functools.partial(tendencies, lo - base), 0)
            base += hi - lo + 1

        total = -(-6 * count // PAIR)
        units = 2 if total == 4 else 3

        def circle_filter(p, carry):
            wave = lax.broadcasted_iota(jnp.int32, (PAIR, 2 * LANES), 1)
            wave = RADIX * jnp.where(wave >= LANES, wave - LANES, wave)

            def place(unit, a, half):
                d, s = a // SUB, a % SUB
                start = (d * TILE_ROWS + (p * units + unit) * PAIR + half * SUB) * SUB + s
                return pl.ds(start, SUB, stride=SUB)

            def cut_of(unit):
                at = pl.multiple_of((p * units + unit) * PAIR, PAIR)
                return cut_ref[3 * outer + index, pl.ds(at, PAIR), :]

            def analyse(unit, half):
                re, im = real_fft([t_ref[place(unit, a, half), :] for a in range(RADIX)])
                for k in range(HALF + 1):
                    c, s = twc_ref[k : k + 1, :], tws_ref[k : k + 1, :]
                    if k == 0:
                        yr, yi = re[k], jnp.zeros_like(re[k])
                    elif im[k] is None:
                        yr, yi = re[k] * c, -(re[k] * s)
                    else:
                        yr, yi = re[k] * c + im[k] * s, im[k] * c - re[k] * s
                    at = pl.ds((k * 2 + half) * SUB, SUB)
                    y_refs[unit][at, 0:LANES] = yr
                    y_refs[unit][at, LANES : 2 * LANES] = yi

            def product(y, whi, wlo):
                n = y.shape[0]
                hi_part = y.astype(jnp.bfloat16)
                lo_part = (y - hi_part.astype(jnp.float32)).astype(jnp.bfloat16)
                dot = functools.partial(jnp.dot, preferred_element_type=jnp.float32)
                both = dot(jnp.concatenate([hi_part, lo_part], axis=0), whi)
                return both[:n] + both[n:] + dot(hi_part, wlo)

            def mask(unit, start):
                cut = cut_of(unit)
                cut2 = jnp.concatenate([cut, cut], axis=1)
                rows = slice(start * PAIR, (start + BLOCK) * PAIR)
                spec = product(y_refs[unit][rows, :], wfh_ref[...], wfl_ref[...])
                keep = []
                for k in range(start, start + BLOCK):
                    folded = jnp.minimum(wave + k, RADIX * LANES - k - wave)
                    keep.append(folded < cut2)
                spec = jnp.where(jnp.concatenate(keep, axis=0), spec, 0.0)
                y_refs[unit][rows, :] = product(spec, wbh_ref[...], wbl_ref[...])

            def synthesise(unit, half):
                re, im = [], []
                for k in range(HALF + 1):
                    c, s = twc_ref[k : k + 1, :], tws_ref[k : k + 1, :]
                    at = pl.ds((k * 2 + half) * SUB, SUB)
                    yr = y_refs[unit][at, 0:LANES]
                    if k == 0:
                        re.append(yr)
                        im.append(None)
                        continue
                    yi = y_refs[unit][at, LANES : 2 * LANES]
                    re.append(yr * c - yi * s)
                    im.append(None if k == HALF else yr * s + yi * c)
                circles = real_ifft(re, im)
                polar = cut_of(unit)[half * SUB : (half + 1) * SUB] < UNCUT
                for a in range(RADIX):
                    at = place(unit, a, half)
                    t_ref[at, :] = jnp.where(polar, circles[a], t_ref[at, :])

            for unit in range(units):
                for half in range(2):
                    analyse(unit, half)
            for start in range(0, HALF + 1, BLOCK):
                for unit in range(units):
                    mask(unit, start)
            for unit in range(units):
                for half in range(2):
                    synthesise(unit, half)
            return carry

        @pl.when(flags[3 * outer + index] > 0)
        def _():
            lax.fori_loop(0, -(-total // units), circle_filter, 0)

        def update(shift, r, carry):
            inside = coef[6, r]
            for f in range(6):
                for d in range(chunks):
                    start = (d * TILE_ROWS + (r - shift) * 6 + f) * SUB
                    change = t_ref[pl.ds(pl.multiple_of(start, SUB), SUB), :]
                    value = inside * (x_ref[d, r * 7 + f] + (fraction * step_size) * change)
                    if final:
                        out_ref[d, (r - shift) * 6 + f] = value
                    else:
                        dst[d, r * 6 + f] = value
            return carry

        spans = ranges[index]
        if final and not outer:
            (lo, hi), middle = spans[0], spans[0][0] + out_edges[1]
            spans = ((lo, middle - 1), (middle, hi))
        base = 0
        for i, (lo, hi) in enumerate(spans):
            lax.fori_loop(lo, hi + 1, functools.partial(update, lo - base), 0)
            base += hi - lo + 1
            if final:
                departure(i).start()
        if not final and not outer:
            for copy in edges(index):
                copy.start()

    stage(x_ref, s1_ref, 0, 1.0 / 3.0)
    stage(s1_ref, s2_ref, 1, 0.5)
    stage(s2_ref, None, 2, 1.0)
    for i in range(2):
        departure(i).wait()
        if not outer:
            for copy in edges(i):
                copy.wait()


def row_tables(cutoffs, row_start, height, total_rows, polar):
    row_ids = row_start - HALO + jnp.arange(height, dtype=jnp.int32)
    spacing = math.pi / total_rows
    centre_lat = -0.5 * math.pi + (row_ids.astype(jnp.float32) + 0.5) * spacing
    face_lat = -0.5 * math.pi + (row_ids.astype(jnp.float32) + 1.0) * spacing
    inside = jnp.where((row_ids >= 0) & (row_ids < total_rows), 1.0, 0.0).astype(jnp.float32)
    live = jnp.where((row_ids >= 0) & (row_ids < total_rows - 1), 1.0, 0.0).astype(jnp.float32)
    centre_cos = jnp.cos(centre_lat)
    face_cos = jnp.cos(face_lat) * live
    face_inverse = live / (face_cos + (1.0 - live))
    coef = jnp.stack(
        [centre_cos, 1.0 / centre_cos, face_inverse, jnp.sin(face_lat), face_cos, live, inside]
    )
    capped = ((row_ids >= 0) & (row_ids < polar)) | (
        (row_ids >= total_rows - polar) & (row_ids < total_rows)
    )
    position = jnp.where(row_ids < polar, row_ids, row_ids - (total_rows - 2 * polar))
    table_ids = jnp.arange(2 * polar, dtype=jnp.int32)
    cut = jnp.sum(
        jnp.where(position[:, None] == table_ids[None, :], cutoffs[None, :], 0), axis=1, dtype=jnp.int32
    )
    cut = jnp.where(capped, cut, UNCUT)
    stages = []
    for outer in (False, True):
        for spans in stage_rows(height, outer):
            rows = jnp.repeat(jnp.concatenate([cut[lo : hi + 1] for lo, hi in spans]), 6)
            stages.append(jnp.pad(rows, (0, TILE_ROWS - rows.shape[0]), constant_values=UNCUT))
    cuts = jnp.stack(stages)
    flags = jnp.any(cuts < UNCUT, axis=1).astype(jnp.int32)
    return coef, flags, jnp.broadcast_to(cuts[:, :, None], (6, TILE_ROWS, LANES))


def body(thickness, winds, terrain, cutoffs):
    row_count, col_count = thickness.shape[1], thickness.shape[2]
    bands, sectors = lax.axis_size("lat"), lax.axis_size("lon")
    total_rows, circle = row_count * bands, col_count * sectors
    polar = (total_rows + 2) // 6
    own = row_count // sectors
    height = own + 2 * HALO
    merid_step = circle / (2.0 * total_rows)
    step_size = 0.1 * min(1.0, merid_step)
    lat = lax.axis_index("lat")
    flat = winds.reshape(4, row_count, col_count)

    vmem = pl.BlockSpec(memory_space=pltpu.VMEM)
    smem = pl.BlockSpec(memory_space=pltpu.SMEM)
    hbm = pl.BlockSpec(memory_space=pltpu.HBM)
    rim = jax.ShapeDtypeStruct((HALO * 7 * SUB, LANES), jnp.float32)
    tail, head = pl.pallas_call(
        edge_kernel,
        out_shape=(rim, rim),
        in_specs=[hbm] * 3,
        out_specs=(vmem, vmem),
        scratch_shapes=[
            pltpu.VMEM((2, 7, SUB, col_count), jnp.float32),
            pltpu.SemaphoreType.DMA((2, 7)),
        ],
        name="edge",
    )(thickness, flat, terrain)
    south = lax.ppermute(tail, "lat", [(i, i + 1) for i in range(bands - 1)])
    north = lax.ppermute(head, "lat", [(i + 1, i) for i in range(bands - 1)])

    def piece(rows, fields):
        return jax.ShapeDtypeStruct((sectors, rows * fields * SUB, LANES), jnp.float32)

    def pack(outer):
        out = piece(height - INNER if outer else INNER, 7)
        return pl.pallas_call(
            functools.partial(pack_kernel, outer, bands),
            out_shape=out,
            in_specs=[smem] + [hbm] * 3,
            out_specs=hbm,
            scratch_shapes=[
                pltpu.VMEM(thickness.shape, jnp.float32),
                pltpu.VMEM(flat.shape, jnp.float32),
                pltpu.VMEM(terrain.shape, jnp.float32),
                pltpu.VMEM(out.shape, jnp.float32),
                pltpu.SemaphoreType.DMA((3, sectors)),
                pltpu.SemaphoreType.DMA((sectors,)),
            ],
            compiler_params=pltpu.CompilerParams(vmem_limit_bytes=56 << 20),
            cost_estimate=pl.CostEstimate(flops=0, bytes_accessed=12 << 20, transcendentals=0),
            name="pack_outer" if outer else "pack_inner",
        )(lat.reshape(1).astype(jnp.int32), thickness, flat, terrain)

    packed_low = pack(False)
    packed_high = pack(True)
    packed_high = pl.pallas_call(
        rim_kernel,
        out_shape=jax.ShapeDtypeStruct(packed_high.shape, jnp.float32),
        in_specs=[vmem, vmem, hbm],
        out_specs=hbm,
        scratch_shapes=[pltpu.SemaphoreType.DMA((2,))],
        input_output_aliases={2: 0},
        name="rim",
    )(south, north, packed_high)
    row_start = lat * row_count + lax.axis_index("lon") * own
    coef, flags, cuts = row_tables(cutoffs, row_start, height, total_rows, polar)
    packed_high, coef, flags, cuts = lax.optimization_barrier((packed_high, coef, flags, cuts))
    circles_low = lax.all_to_all(packed_low, "lon", 0, 0)
    circles_high = lax.all_to_all(packed_high, "lon", 0, 0)

    tables = [jnp.asarray(t) for t in filter_tables()]
    edges = jax.ShapeDtypeStruct((sectors, 24, SUB, LANES), jnp.float32)

    def step(outer, states, saved):
        rows = sum(hi - lo + 1 for lo, hi in stage_rows(height, outer)[2])
        out = jax.ShapeDtypeStruct((sectors, 6 * rows, SUB, LANES), jnp.float32)
        states = [x.reshape(sectors, -1, SUB, LANES) for x in states]
        return pl.pallas_call(
            functools.partial(step_kernel, outer, height, merid_step, step_size),
            out_shape=out if outer else (out, edges, edges),
            in_specs=[smem, smem] + [hbm] * len(states + saved) + [vmem] * 7,
            out_specs=hbm if outer else (hbm, hbm, hbm),
            scratch_shapes=[
                pltpu.VMEM((sectors, 7 * height, SUB, LANES), jnp.float32),
                pltpu.VMEM((sectors, 6 * height, SUB, LANES), jnp.float32),
                pltpu.VMEM((sectors, 6 * height, SUB, LANES), jnp.float32),
                pltpu.VMEM(out.shape, jnp.float32),
                pltpu.VMEM((sectors * TILE_ROWS * SUB, LANES), jnp.float32),
                pltpu.SemaphoreType.DMA((4,)),
                pltpu.SemaphoreType.DMA((2,)),
                pltpu.SemaphoreType.DMA((2, 2)),
            ]
            + [pltpu.VMEM((height * 2 * sectors, SUB, LANES), jnp.float32)] * 4
            + [pltpu.VMEM(((HALF + 1) * PAIR, 2 * LANES), jnp.float32)] * UNITS,
            compiler_params=pltpu.CompilerParams(vmem_limit_bytes=54 << 20),
            cost_estimate=pl.CostEstimate(flops=0, bytes_accessed=64 << 20, transcendentals=0),
            name="step_outer" if outer else "step_inner",
        )(coef, flags, *states, *saved, cuts, *tables)

    new_low, *saved = step(False, [circles_low], [])
    returned_low = lax.all_to_all(new_low.reshape(sectors, -1, LANES), "lon", 0, 0)
    new_high = step(True, [circles_low, circles_high], saved)
    returned_low, new_high = lax.optimization_barrier((returned_low, new_high))
    returned_high = lax.all_to_all(new_high.reshape(sectors, -1, LANES), "lon", 0, 0)

    new_thickness, new_winds = pl.pallas_call(
        unpack_kernel,
        out_shape=(
            jax.ShapeDtypeStruct(thickness.shape, jnp.float32),
            jax.ShapeDtypeStruct(flat.shape, jnp.float32),
        ),
        in_specs=[vmem, vmem],
        out_specs=(hbm, hbm),
        scratch_shapes=[
            pltpu.VMEM((6, row_count, col_count), jnp.float32),
            pltpu.SemaphoreType.DMA((6,)),
        ],
        compiler_params=pltpu.CompilerParams(vmem_limit_bytes=40 << 20),
        name="unpack",
    )(returned_low, returned_high)
    return new_thickness, new_winds.reshape(winds.shape)


def solution(mesh):
    in_specs = (P(None, "lat", "lon"), P(None, None, "lat", "lon"), P("lat", "lon"), P())
    out_specs = (P(None, "lat", "lon"), P(None, None, "lat", "lon"))
    return jax.shard_map(body, mesh=mesh, in_specs=in_specs, out_specs=out_specs, check_vma=False)
```
